32 devices in a mesh: case: 2 (over x), ax: 16 (over z, y, core).
Axes of the slice: x: 2, y: 2, z: 4, core: 2. Of those that a mesh axis runs over, the one named last changes fastest.
Arguments:
- populations: float32 [19, 32, 128, 128], P(None, 'ax', 'case'), parts along dimension 2, may hold values from 0 to 1, as said below
- solid_mask: int32 [32, 128, 128], P('ax', 'case'), parts along dimension 1, may hold values from 0 to 1, as said below
- link_flags: int32 [2, 32, 128, 128], P(None, 'ax', 'case'), parts along dimension 2, may hold values from 0 to 511, as said below
- inlet_cells: int32 [1024], P('case'), parts along dimension 0, may hold values from 0 to 8191, as said below
- pod_basis: float32 [512, 3, 512], P(None, None, 'ax'), may hold values from -0.15625 to 0.15625
- mri_frames: float32 [24, 6, 512], P(None, 'case', 'ax'), parts along dimension 1
- frame_index: int32 [1], replicated, may hold values from 0 to 23
Outputs:
- advanced_populations: float32 [19, 32, 128, 128], P(None, 'ax', 'case'), parts along dimension 2
- inflow: float32 [2, 6, 512], P(None, 'case', 'ax'), parts along dimension 1
The draws below stay inside these ranges and needn't reach their ends.
There are 2 independent parts, one for each index of `case`. The reference program is written for one: setup_inputs(seed, part) draws one part's arguments, and reference() takes and returns one part's arrays. A program takes and returns all parts, laid end to end along the dimension named above; an argument that names none is the same for every part. Nothing has to cross between parts.
Inputs may be any that keep to these rules, and one draw needn't show every extreme that they name: `solid_mask`: 1 marks a wall cell, 0 a fluid cell; the two outermost rows and columns of every cross-section are wall cells. `link_flags`: at a fluid cell, bit (i - 1) mod 9 of word (i - 1) div 9 is set exactly when the cell at minus c_i is a wall cell, the grid being continued past its first and last plane by repeating those planes; zero at wall cells. `inlet_cells`: distinct cells of the first plane, all of them fluid cells. `populations`: every entry is positive.
All inputs are finite; a program needn't handle non-finite values.
Results may differ from the reference program's by a relative error of at most 0.00011.
Values sent between devices are 32-bit elements; how exact they have to be, the bound alone decides.
A program may use at most 64 MiB of HBM per device.

```python
import math
import jax
import jax.numpy as jnp
from jax import lax

NYC = 64
NXC = 128
MODES = 512
FRAMES = 24
STEPS = 2
NZ = 32
NIN = 512


lattice_c = ((0, 0, 0), (1, 0, 0), (-1, 0, 0), (0, 1, 0), (0, -1, 0), (0, 0, 1), (0, 0, -1), (1, 1, 0), (-1, -1, 0), (1, -1, 0), (-1, 1, 0), (1, 0, 1), (-1, 0, -1), (1, 0, -1), (-1, 0, 1), (0, 1, 1), (0, -1, -1), (0, 1, -1), (0, -1, 1))


lattice_w = (1.0 / 3.0,) + (1.0 / 18.0,) * 6 + (1.0 / 36.0,) * 12


def vessel_fluid(key):
    geo_key = jax.random.fold_in(key, 7071)
    key_center, key_jitter = jax.random.split(geo_key)
    center_z = jax.random.randint(key_center, (), NZ // 4, NZ - NZ // 4)
    half_len = max(NZ // 8, 1)
    radius = min(NYC, NXC) // 2 - 3
    shape_all = (NZ, NYC, NXC)
    axial_pos = lax.broadcasted_iota(jnp.int32, shape_all, 0)
    across_y = lax.broadcasted_iota(jnp.int32, shape_all, 1) - NYC // 2
    across_x = lax.broadcasted_iota(jnp.int32, shape_all, 2) - NXC // 2
    narrowing = jnp.maximum(half_len - jnp.abs(axial_pos - center_z), 0)
    threshold_sq = radius * radius - radius * radius * 6 * narrowing // (10 * half_len)
    jitter = jax.random.randint(key_jitter, shape_all, -radius, radius + 1)
    return (across_x * across_x + across_y * across_y < threshold_sq + jitter).astype(jnp.int32)


def draw_solid_mask(key, part):
    return 1 - vessel_fluid(key)


def draw_link_flags(key, part):
    fluid = vessel_fluid(key)
    extended = jnp.concatenate([fluid[:1], fluid, fluid[-1:]], axis=0)
    walled = 1 - extended
    planes_all = fluid.shape[0]
    low_word = jnp.zeros_like(fluid)
    high_word = jnp.zeros_like(fluid)
    for direction in range(1, 19):
        step_x, step_y, step_z = lattice_c[direction]
        behind = walled[1 - step_z:1 - step_z + planes_all]
        behind = jnp.roll(behind, (step_y, step_x), axis=(1, 2))
        term = fluid * behind * 2 ** ((direction - 1) % 9)
        if direction <= 9:
            low_word = low_word + term
        else:
            high_word = high_word + term
    return jnp.stack([low_word, high_word])


def draw_inlet_cells(key, part):
    fluid_first = vessel_fluid(key)[0].reshape(-1)
    plane_cells = NYC * NXC
    ordering = jax.random.permutation(jax.random.fold_in(key, 9091), plane_cells).astype(jnp.int32)
    ranks = jnp.zeros((plane_cells,), jnp.int32).at[ordering].set(jnp.arange(plane_cells, dtype=jnp.int32))
    scores = (1 - fluid_first) * plane_cells + ranks
    return jnp.argsort(scores, stable=True)[:NIN].astype(jnp.int32)


def draw_populations(key, part):
    key_density, key_velocity, key_noise = jax.random.split(jax.random.fold_in(key, 3301), 3)
    shape_cells = (NZ, NYC, NXC)
    density = 1.0 + 0.05 * jax.random.truncated_normal(key_density, -2.5, 2.5, shape_cells, jnp.float32)
    velocity = 0.03 * jax.random.truncated_normal(key_velocity, -2.5, 2.5, (3,) + shape_cells, jnp.float32)
    noise = 0.16 * jax.random.truncated_normal(key_noise, -2.5, 2.5, (19,) + shape_cells, jnp.float32)
    speed_sq = velocity[0] * velocity[0] + velocity[1] * velocity[1] + velocity[2] * velocity[2]
    listed = []
    for direction in range(19):
        step_x, step_y, step_z = lattice_c[direction]
        along = step_x * velocity[0] + step_y * velocity[1] + step_z * velocity[2]
        equil_part = density * (1.0 + 3.0 * along + 4.5 * along * along - 1.5 * speed_sq)
        listed.append(lattice_w[direction] * (equil_part + noise[direction]))
    return jnp.stack(listed)


def draw_mri_frames(key, part):
    shape_all = (FRAMES, 3, NIN)
    frame_key, value_key = jax.random.split(jax.random.fold_in(key, 5501))
    position = lax.broadcasted_iota(jnp.int32, shape_all, 2).astype(jnp.float32) / NIN
    rising = 1.0 + 2.0 * position
    values = jax.random.truncated_normal(value_key, -4.0, 4.0, shape_all, jnp.float32) * rising
    return values


def block_levels(own_key, shape, shards, low, largest):
    level, own = 1.0, jax.random.fold_in(own_key, 6)
    for axis_at, parts in shards:
        heights = jnp.exp(jax.random.uniform(jax.random.fold_in(own, axis_at), (parts,), jnp.float32, low / len(shards), largest / len(shards)))
        level = level * jnp.repeat(heights, shape[axis_at] // parts).reshape([-1 if axis == axis_at else 1 for axis in range(len(shape))])
    return level


def gaussian(key, shape, deviation, bound, shards=(), held_as=jnp.bfloat16):
    result = jax.random.normal(key, shape, jnp.float32) * deviation
    if len(shards) > 0:
        result = block_levels(key, shape, shards, -0.22, 0.18) * result
    return jnp.clip(result, min=-bound, max=bound).astype(held_as)


def setup_inputs(seed: int = 0, part: int = 0) -> dict:
    keys = jax.random.split(jax.random.key(seed), 8)
    part_keys = jax.random.split(jax.random.fold_in(keys[7], part), 8)
    populations = draw_populations(jax.random.fold_in(jax.random.fold_in(keys[7], part), 71), part)
    solid_mask = draw_solid_mask(jax.random.fold_in(jax.random.fold_in(keys[7], part), 71), part)
    link_flags = draw_link_flags(jax.random.fold_in(jax.random.fold_in(keys[7], part), 71), part)
    inlet_cells = draw_inlet_cells(jax.random.fold_in(jax.random.fold_in(keys[7], part), 71), part)
    pod_basis = gaussian(keys[4], (MODES, 3, NIN), (3 * NIN) ** -0.5, 0.15625, ((2, 16),), jnp.float32)
    mri_frames = draw_mri_frames(jax.random.fold_in(jax.random.fold_in(keys[7], part), 71), part)
    frame_index = jax.random.randint(keys[6], (1,), 0, FRAMES).astype(jnp.int32)
    return {"populations": populations, "solid_mask": solid_mask, "link_flags": link_flags, "inlet_cells": inlet_cells, "pod_basis": pod_basis, "mri_frames": mri_frames, "frame_index": frame_index}


lattice_c = ((0, 0, 0), (1, 0, 0), (-1, 0, 0), (0, 1, 0), (0, -1, 0), (0, 0, 1), (0, 0, -1), (1, 1, 0), (-1, -1, 0), (1, -1, 0), (-1, 1, 0), (1, 0, 1), (-1, 0, -1), (1, 0, -1), (-1, 0, 1), (0, 1, 1), (0, -1, -1), (0, 1, -1), (0, -1, 1))
lattice_w = (1.0 / 3.0,) + (1.0 / 18.0,) * 6 + (1.0 / 36.0,) * 12
opposite_of = (0, 2, 1, 4, 3, 6, 5, 8, 7, 10, 9, 12, 11, 14, 13, 16, 15, 18, 17)
pair_list = ((0, 0), (1, 1), (2, 2), (0, 1), (0, 2), (1, 2))
relax_base = 0.52
smagorinsky_sq = 0.04
inflow_scale = 0.05

def moment_rows():
    listed = [[1.0] * 19]
    for axis_a in range(3):
        listed.append([float(vector[axis_a]) for vector in lattice_c])
    for pair_a, pair_b in pair_list:
        listed.append([float(vector[pair_a] * vector[pair_b]) for vector in lattice_c])
    return jnp.asarray(listed, dtype=jnp.float32)

def equilibrium(density, velocity):
    lattice = jnp.asarray([[float(entry) for entry in vector] for vector in lattice_c], dtype=jnp.float32)
    weights = jnp.asarray(list(lattice_w), dtype=jnp.float32).reshape((19,) + (1,) * density.ndim)
    projected = jnp.einsum('iq,q...->i...', lattice, velocity, precision=lax.Precision.HIGHEST)
    speed_sq = lax.optimization_barrier(jnp.sum(velocity * velocity, axis=0))
    return weights * density[None] * (1.0 + 3.0 * projected + 4.5 * projected * projected - 1.5 * speed_sq[None])

def collide(populations, solid_mask):
    moments = jnp.einsum('mi,i...->m...', moment_rows(), populations, precision=lax.Precision.HIGHEST)
    density = moments[0]
    velocity = moments[1:4] / density[None]
    nonequil = populations - equilibrium(density, velocity)
    stress = jnp.einsum('mi,i...->m...', moment_rows()[4:], nonequil, precision=lax.Precision.HIGHEST)
    magnitude = stress[0] * stress[0] + stress[1] * stress[1] + stress[2] * stress[2]
    magnitude = magnitude + 2.0 * (stress[3] * stress[3] + stress[4] * stress[4] + stress[5] * stress[5])
    relax_time = 0.5 * (relax_base + jnp.sqrt(relax_base * relax_base + 18.0 * math.sqrt(2.0) * smagorinsky_sq * jnp.sqrt(magnitude) / density))
    relaxed = populations - nonequil / relax_time[None]
    return jnp.where(solid_mask[None] == 1, populations, relaxed)

def stream(relaxed, ghost_low, ghost_high, link_flags, solid_mask):
    padded = jnp.concatenate([ghost_low[:, None], relaxed, ghost_high[:, None]], axis=1)
    planes_here = relaxed.shape[1]
    read = []
    for direction in range(19):
        step_x, step_y, step_z = lattice_c[direction]
        source = padded[direction, 1 - step_z:1 - step_z + planes_here]
        source = jnp.roll(source, (step_y, step_x), axis=(1, 2))
        if direction > 0:
            word = link_flags[(direction - 1) // 9]
            linked = jnp.bitwise_and(jnp.right_shift(word, (direction - 1) % 9), 1)
            source = jnp.where(linked == 1, relaxed[opposite_of[direction]], source)
        read.append(jnp.where(solid_mask == 1, relaxed[direction], source))
    return jnp.stack(read)

def inlet_plane(speeds, inlet_cells, height, plane_width):
    inlet_speed = jnp.zeros((3, height * plane_width), jnp.float32).at[:, inlet_cells].set(speeds)
    inlet_speed = inlet_speed.reshape(3, height, plane_width)
    return equilibrium(jnp.ones((height, plane_width), jnp.float32), inlet_speed)

def reference(populations, solid_mask, link_flags, inlet_cells, pod_basis, mri_frames, frame_index):
    chosen = jnp.stack([mri_frames[(frame_index[0] + segment_index) % FRAMES] for segment_index in range(STEPS)])
    coefficients = jnp.einsum('kjc,sjc->sk', pod_basis, chosen, precision=lax.Precision.HIGHEST)
    inflow = jnp.einsum('kjc,sk->sjc', pod_basis, coefficients, precision=lax.Precision.HIGHEST)
    height = populations.shape[2]
    plane_width = populations.shape[3]
    for segment_index in range(STEPS):
        relaxed = collide(populations, solid_mask)
        ghost_low = inlet_plane(inflow_scale * inflow[segment_index], inlet_cells, height, plane_width)
        populations = stream(relaxed, ghost_low, relaxed[:, -1], link_flags, solid_mask)
    return (populations, inflow)
```

```python
import functools
import math

import jax
import jax.numpy as jnp
from jax import lax
from jax.experimental import pallas as pl
from jax.experimental.pallas import tpu as pltpu
from jax.sharding import PartitionSpec as P

STEPS = 2
MESH = pl.DeviceIdType.MESH
HIGHEST = lax.Precision.HIGHEST
PAD = 8
LANES = 128

lattice_c = (
    (0, 0, 0),
    (1, 0, 0),
    (-1, 0, 0),
    (0, 1, 0),
    (0, -1, 0),
    (0, 0, 1),
    (0, 0, -1),
    (1, 1, 0),
    (-1, -1, 0),
    (1, -1, 0),
    (-1, 1, 0),
    (1, 0, 1),
    (-1, 0, -1),
    (1, 0, -1),
    (-1, 0, 1),
    (0, 1, 1),
    (0, -1, -1),
    (0, 1, -1),
    (0, -1, 1),
)
lattice_w = (1.0 / 3.0,) + (1.0 / 18.0,) * 6 + (1.0 / 36.0,) * 12
opposite_of = (0, 2, 1, 4, 3, 6, 5, 8, 7, 10, 9, 12, 11, 14, 13, 16, 15, 18, 17)
relax_base = 0.52
smagorinsky_sq = 0.04
inflow_scale = 0.05

up_dirs = tuple(i for i in range(19) if lattice_c[i][2] == 1)
down_dirs = tuple(i for i in range(19) if lattice_c[i][2] == -1)
flat_dirs = tuple(i for i in range(19) if lattice_c[i][2] == 0)
slot_of = {d: k for k, d in enumerate(up_dirs + down_dirs + flat_dirs)}
CROSS = len(up_dirs)


def relax(f, solid):
    pair = [f[i] + f[i + 1] for i in range(1, 19, 2)]
    diff = [f[i] - f[i + 1] for i in range(1, 19, 2)]
    in_xy = pair[3] + pair[4]
    in_xz = pair[5] + pair[6]
    in_yz = pair[7] + pair[8]
    density = (f[0] + pair[0]) + (pair[1] + pair[2]) + (in_xy + in_xz) + in_yz
    flux = (
        diff[0] + (diff[3] + diff[4]) + (diff[5] + diff[6]),
        diff[1] + (diff[3] - diff[4]) + (diff[7] + diff[8]),
        diff[2] + (diff[5] - diff[6]) + (diff[7] - diff[8]),
    )
    inverse = 1.0 / density
    speed = [j * inverse for j in flux]
    third = density * (1.0 / 3.0)
    square = [j * u for j, u in zip(flux, speed)]
    s_xx = pair[0] + in_xy + in_xz - third - square[0]
    s_yy = pair[1] + in_xy + in_yz - third - square[1]
    s_zz = pair[2] + in_xz + in_yz - third - square[2]
    s_xy = pair[3] - pair[4] - flux[0] * speed[1]
    s_xz = pair[5] - pair[6] - flux[0] * speed[2]
    s_yz = pair[7] - pair[8] - flux[1] * speed[2]
    magnitude = (s_xx * s_xx + s_yy * s_yy + s_zz * s_zz) + 2.0 * (
        s_xy * s_xy + s_xz * s_xz + s_yz * s_yz
    )
    root = jnp.sqrt(
        relax_base * relax_base
        + (18.0 * math.sqrt(2.0) * smagorinsky_sq) * jnp.sqrt(magnitude) * inverse
    )
    rate = jnp.where(solid == 1, 0.0, 2.0 / (relax_base + root))
    keep = 1.0 - rate
    base = density - 1.5 * (square[0] + square[1] + square[2])
    by_axis = rate * (1.0 / 18.0)
    by_edge = rate * (1.0 / 36.0)
    triple = [3.0 * j for j in flux]
    out = [keep * f[0] + (rate * (1.0 / 3.0)) * base]
    for i in range(1, 19, 2):
        c = lattice_c[i]
        along = moved = None
        for axis in range(3):
            if c[axis] == 0:
                continue
            if along is None:
                along, moved = speed[axis], triple[axis]
            elif c[axis] > 0:
                along, moved = along + speed[axis], moved + triple[axis]
            else:
                along, moved = along - speed[axis], moved - triple[axis]
        even = base + 1.5 * (moved * along)
        weight = by_axis if i < 7 else by_edge
        out.append(keep * f[i] + weight * (even + moved))
        out.append(keep * f[i + 1] + weight * (even - moved))
    return out


def kernel(
    n,
    frame_ref,
    f_hbm,
    solid_hbm,
    flags_hbm,
    cells_ref,
    pod_ref,
    mri_ref,
    out_hbm,
    inflow_ref,
    f_buf,
    solid_buf,
    flags_buf,
    r_buf,
    low,
    high,
    part_send,
    part_recv,
    line_send,
    line_recv,
    in_sem,
    mask_sem,
    out_sem,
    part_ssem,
    part_rsem,
    line_ssem,
    line_rsem,
    up_ssem,
    up_rsem,
    down_ssem,
    down_rsem,
):
    planes, height, width = solid_buf.shape
    steps = STEPS
    frames = mri_ref.shape[1]
    local = mri_ref.shape[2]
    modes = pod_ref.shape[2]
    rep = LANES // local
    groups = n // rep
    chunk = 16
    rows = slice(PAD, PAD + height)
    me = lax.axis_index("ax")

    barrier = pltpu.get_barrier_semaphore()

    def greet(k, carry):
        pl.semaphore_signal(
            barrier, inc=1, device_id={"ax": lax.rem(me + k, n)}, device_id_type=MESH
        )
        return carry

    lax.fori_loop(1, n, greet, 0)

    loads = []
    for z in range(planes):
        loads.append(pltpu.make_async_copy(f_hbm.at[:, z], f_buf.at[:, z], in_sem.at[z]))
    solid_load = pltpu.make_async_copy(solid_hbm, solid_buf, mask_sem.at[0])
    flags_load = pltpu.make_async_copy(flags_hbm, flags_buf, mask_sem.at[1])
    loads[planes - 1].start()
    solid_load.start()
    for z in range(planes - 2, -1, -1):
        loads[z].start()
    flags_load.start()

    row_at = lax.broadcasted_iota(jnp.int32, (8, local), 0)
    frame_at = lax.broadcasted_iota(jnp.int32, (frames, local), 0)
    partial = jnp.zeros((8, modes), jnp.float32)
    for j in range(3):
        chosen = jnp.zeros((8, local), jnp.float32)
        for s in range(steps):
            frame = lax.rem(frame_ref[0] + s, frames)
            line = jnp.sum(jnp.where(frame_at == frame, mri_ref[j], 0.0), axis=0, keepdims=True)
            chosen = jnp.where(row_at == s, line, chosen)
        partial = partial + jnp.dot(
            chosen, pod_ref[j], precision=HIGHEST, preferred_element_type=jnp.float32
        )
    part_send[...] = partial[:steps]
    part_recv[me] = partial[:steps]

    def collide(s, z):
        def at(c, carry):
            r0 = pl.multiple_of(c * chunk, chunk)
            here = pl.ds(r0, chunk)
            there = pl.ds(pl.multiple_of(r0 + PAD, 8), chunk)
            f = [f_buf[i, z, here, :] for i in range(19)]
            relaxed = relax(f, solid_buf[z, here, :])
            for i in range(19):
                r_buf[s, slot_of[i], z, there, :] = relaxed[i]
            return carry

        lax.fori_loop(0, height // chunk, at, 0)

    def up_copy(s):
        return pltpu.make_async_remote_copy(
            src_ref=r_buf.at[s, pl.ds(0, CROSS), planes - 1, pl.ds(PAD, height)],
            dst_ref=low.at[s, :, pl.ds(PAD, height)],
            send_sem=up_ssem.at[s],
            recv_sem=up_rsem.at[s],
            device_id={"ax": lax.rem(me + 1, n)},
            device_id_type=MESH,
        )

    def down_copy(s):
        return pltpu.make_async_remote_copy(
            src_ref=r_buf.at[s, pl.ds(CROSS, CROSS), 0, pl.ds(PAD, height)],
            dst_ref=high.at[s, :, pl.ds(PAD, height)],
            send_sem=down_ssem.at[s],
            recv_sem=down_rsem.at[s],
            device_id={"ax": lax.rem(me + n - 1, n)},
            device_id_type=MESH,
        )

    def part_copy(k):
        return pltpu.make_async_remote_copy(
            src_ref=part_send,
            dst_ref=part_recv.at[me],
            send_sem=part_ssem.at[k],
            recv_sem=part_rsem.at[me],
            device_id={"ax": lax.rem(me + k, n)},
            device_id_type=MESH,
        )

    def part_arrival(source):
        return pltpu.make_async_remote_copy(
            src_ref=part_send,
            dst_ref=part_recv.at[source],
            send_sem=part_ssem.at[0],
            recv_sem=part_rsem.at[source],
            device_id={"ax": lax.rem(me + 1, n)},
            device_id_type=MESH,
        )

    def line_copy(source):
        return pltpu.make_async_remote_copy(
            src_ref=line_send,
            dst_ref=line_recv.at[source],
            send_sem=line_ssem.at[0],
            recv_sem=line_rsem.at[source],
            device_id={"ax": 0},
            device_id_type=MESH,
        )

    def send_up(s):
        @pl.when(me < n - 1)
        def _():
            up_copy(s).start()

    def send_down(s):
        @pl.when(me > 0)
        def _():
            down_copy(s).start()

    def stream(s, z, dirs):
        solid = solid_buf[z] == 1
        for i in dirs:
            step_x, step_y, step_z = lattice_c[i]
            own = r_buf[s, slot_of[i], z, rows, :]
            if i == 0:
                f_buf[i, z] = own
                continue
            moved = slice(PAD - step_y, PAD - step_y + height)
            if 0 <= z - step_z < planes:
                source = r_buf[s, slot_of[i], z - step_z, moved, :]
            elif step_z > 0:
                source = low[s, slot_of[i], moved, :]
            else:
                source = high[s, slot_of[i] - CROSS, moved, :]
            if step_x != 0:
                source = pltpu.roll(source, step_x % width, 1)
            bit = 1 << ((i - 1) % 9)
            linked = (flags_buf[(i - 1) // 9, z] & bit) != 0
            back = r_buf[s, slot_of[opposite_of[i]], z, rows, :]
            f_buf[i, z] = jnp.where(solid, own, jnp.where(linked, back, source))

    def inlet():
        def arrived(k, carry):
            line_copy(k).wait_recv()
            return carry

        lax.fori_loop(1, n, arrived, 0)
        lines = [
            functools.reduce(jnp.add, [line_recv[g * rep + k] for k in range(rep)])
            for g in range(groups)
        ]
        cells = cells_ref[...]
        count = cells.shape[1]
        if width & (width - 1) == 0:
            cell_y = lax.shift_right_logical(cells, width.bit_length() - 1)
            cell_x = cells & (width - 1)
        else:
            cell_y = cells // width
            cell_x = cells - cell_y * width
        at_y = lax.broadcasted_iota(jnp.int32, (height, count), 0) == cell_y
        at_x = lax.broadcasted_iota(jnp.int32, (width, count), 0) == cell_x
        spread = jnp.concatenate(
            [
                jnp.where(
                    at_y, jnp.concatenate([v[j, s : s + 1, :] for v in lines], axis=1), 0.0
                )
                for s in range(steps)
                for j in range(3)
            ],
            axis=0,
        )
        plane = lax.dot_general(
            spread,
            jnp.where(at_x, 1.0, 0.0),
            (((1,), (1,)), ((), ())),
            precision=HIGHEST,
            preferred_element_type=jnp.float32,
        )
        for s in range(steps):
            v = [
                inflow_scale * plane[(3 * s + j) * height : (3 * s + j + 1) * height]
                for j in range(3)
            ]
            speed_sq = v[0] * v[0] + v[1] * v[1] + v[2] * v[2]
            for k, i in enumerate(up_dirs):
                along = v[2]
                for axis in range(2):
                    if lattice_c[i][axis] > 0:
                        along = along + v[axis]
                    elif lattice_c[i][axis] < 0:
                        along = along - v[axis]
                low[s, k, rows, :] = lattice_w[i] * (
                    1.0 + 3.0 * along + 4.5 * along * along - 1.5 * speed_sq
                )

    loads[planes - 1].wait()
    solid_load.wait()
    collide(0, planes - 1)
    pl.semaphore_wait(barrier, n - 1)

    def part_start(k, carry):
        part_copy(k).start()
        return carry

    lax.fori_loop(1, n, part_start, 0)
    send_up(0)
    for z in range(planes - 2, -1, -1):
        loads[z].wait()
        collide(0, z)
    send_down(0)
    flags_load.wait()

    for s in range(steps):
        last = s == steps - 1
        for z in range(planes - 1, -1, -1):
            early = [
                i
                for i in range(19)
                if lattice_c[i][2] == 0 or 0 <= z - lattice_c[i][2] < planes
            ]
            stream(s, z, early)
        if s == 0:
            def part_wait(k, carry):
                part_arrival(lax.rem(me + k, n)).wait_recv()
                return carry

            lax.fori_loop(1, n, part_wait, 0)
            total = jnp.sum(part_recv[...], axis=0)
            total = jnp.concatenate([total, jnp.zeros((8 - steps, modes), jnp.float32)], axis=0)
            basis = jnp.concatenate([pod_ref[j] for j in range(3) for _ in range(rep)], axis=0)
            lines = lax.dot_general(
                total,
                basis,
                (((1,), (1,)), ((), ())),
                precision=HIGHEST,
                preferred_element_type=jnp.float32,
            )
            lane = lax.broadcasted_iota(jnp.int32, (steps, LANES), 1)
            first = lax.rem(me, rep) * local
            mine = (lane >= first) & (lane < first + local)
            for j in range(3):
                line = lines[:steps, j * LANES : (j + 1) * LANES]
                inflow_ref[j] = line[:, :local]
                line_send[j] = jnp.where(mine, line, 0.0)

            @pl.when(me == 0)
            def _():
                line_recv[0] = line_send[...]

            @pl.when(me > 0)
            def _():
                line_copy(me).start()

        for z in range(planes - 1, -1, -1):
            if z == planes - 1:

                @pl.when(me < n - 1)
                def _():
                    down_copy(s).wait_recv()

                @pl.when(me == n - 1)
                def _():
                    for k in range(CROSS):
                        high[s, k, rows, :] = r_buf[s, CROSS + k, planes - 1, rows, :]

                stream(s, z, down_dirs)
            if z == 0:
                if s == 0:
                    pl.when(me == 0)(inlet)

                @pl.when(me > 0)
                def _():
                    up_copy(s).wait_recv()

                stream(s, z, up_dirs)
            if last:
                pltpu.make_async_copy(f_buf.at[:, z], out_hbm.at[:, z], out_sem.at[z]).start()
            else:
                collide(s + 1, z)
                if z == planes - 1:
                    send_up(s + 1)
                if z == 0:
                    send_down(s + 1)

    def part_done(k, carry):
        part_copy(k).wait_send()
        return carry

    lax.fori_loop(1, n, part_done, 0)

    @pl.when(me > 0)
    def _():
        line_copy(me).wait_send()
        for s in range(steps):
            down_copy(s).wait_send()

    @pl.when(me < n - 1)
    def _():
        for s in range(steps):
            up_copy(s).wait_send()

    for z in range(planes):
        pltpu.make_async_copy(f_buf.at[:, z], out_hbm.at[:, z], out_sem.at[z]).wait()


def body(n, populations, solid_mask, link_flags, inlet_cells, pod_basis, mri_frames, frame_index):
    planes, height, width = solid_mask.shape
    modes, _, local = pod_basis.shape
    if planes < 2 or LANES % local or n % (LANES // local) or width != LANES or height % 16:
        raise ValueError("sizes")
    dma = pltpu.SemaphoreType.DMA
    f32 = jnp.float32
    advanced, inflow = pl.pallas_call(
        functools.partial(kernel, n),
        name="lattice",
        out_shape=(
            jax.ShapeDtypeStruct(populations.shape, f32),
            jax.ShapeDtypeStruct((3, STEPS, local), f32),
        ),
        in_specs=[
            pl.BlockSpec(memory_space=pltpu.SMEM),
            pl.BlockSpec(memory_space=pl.ANY),
            pl.BlockSpec(memory_space=pl.ANY),
            pl.BlockSpec(memory_space=pl.ANY),
            pl.BlockSpec(memory_space=pltpu.VMEM),
            pl.BlockSpec(memory_space=pltpu.VMEM),
            pl.BlockSpec(memory_space=pltpu.VMEM),
        ],
        out_specs=(
            pl.BlockSpec(memory_space=pl.ANY),
            pl.BlockSpec(memory_space=pltpu.VMEM),
        ),
        scratch_shapes=[
            pltpu.VMEM((19, planes, height, width), f32),
            pltpu.VMEM((planes, height, width), jnp.int32),
            pltpu.VMEM((2, planes, height, width), jnp.int32),
            pltpu.VMEM((STEPS, 19, planes, height + 2 * PAD, width), f32),
            pltpu.VMEM((STEPS, CROSS, height + 2 * PAD, width), f32),
            pltpu.VMEM((STEPS, CROSS, height + 2 * PAD, width), f32),
            pltpu.VMEM((STEPS, modes), f32),
            pltpu.VMEM((n, STEPS, modes), f32),
            pltpu.VMEM((3, STEPS, LANES), f32),
            pltpu.VMEM((n, 3, STEPS, LANES), f32),
            dma((planes,)),
            dma((2,)),
            dma((planes,)),
            dma((n,)),
            dma((n,)),
            dma((1,)),
            dma((n,)),
            dma((STEPS,)),
            dma((STEPS,)),
            dma((STEPS,)),
            dma((STEPS,)),
        ],
        compiler_params=pltpu.CompilerParams(collective_id=0, has_side_effects=True),
    )(
        frame_index,
        populations,
        solid_mask,
        link_flags,
        inlet_cells.reshape(1, -1),
        jnp.transpose(pod_basis, (1, 2, 0)),
        jnp.transpose(mri_frames, (1, 0, 2)),
    )
    return advanced, jnp.transpose(inflow, (1, 0, 2))


def solution(mesh):
    in_specs = (
        P(None, "ax", "case", None),
        P("ax", "case", None),
        P(None, "ax", "case", None),
        P("case"),
        P(None, None, "ax"),
        P(None, "case", "ax"),
        P(),
    )
    out_specs = (P(None, "ax", "case", None), P(None, "case", "ax"))
    return jax.shard_map(
        functools.partial(body, mesh.shape["ax"]),
        mesh=mesh,
        in_specs=in_specs,
        out_specs=out_specs,
        check_vma=False,
    )
```

```python
import functools
import math

import jax
import jax.numpy as jnp
from jax import lax
from jax.experimental import pallas as pl
from jax.experimental.pallas import tpu as pltpu
from jax.sharding import PartitionSpec as P

STEPS = 2
MESH = pl.DeviceIdType.MESH
PAD = 8
LANES = 128

lattice_c = (
    (0, 0, 0),
    (1, 0, 0),
    (-1, 0, 0),
    (0, 1, 0),
    (0, -1, 0),
    (0, 0, 1),
    (0, 0, -1),
    (1, 1, 0),
    (-1, -1, 0),
    (1, -1, 0),
    (-1, 1, 0),
    (1, 0, 1),
    (-1, 0, -1),
    (1, 0, -1),
    (-1, 0, 1),
    (0, 1, 1),
    (0, -1, -1),
    (0, 1, -1),
    (0, -1, 1),
)
lattice_w = (1.0 / 3.0,) + (1.0 / 18.0,) * 6 + (1.0 / 36.0,) * 12
opposite_of = (0, 2, 1, 4, 3, 6, 5, 8, 7, 10, 9, 12, 11, 14, 13, 16, 15, 18, 17)
relax_base = 0.52
smagorinsky_sq = 0.04
inflow_scale = 0.05

up_dirs = tuple(i for i in range(19) if lattice_c[i][2] == 1)
down_dirs = tuple(i for i in range(19) if lattice_c[i][2] == -1)
flat_dirs = tuple(i for i in range(19) if lattice_c[i][2] == 0)
slot_of = {d: k for k, d in enumerate(up_dirs + down_dirs + flat_dirs)}
CROSS = len(up_dirs)


def split_dot(left, right, dims):
    dot = functools.partial(
        lax.dot_general, dimension_numbers=dims, preferred_element_type=jnp.float32
    )
    rows = left.shape[0]
    left_high = left.astype(jnp.bfloat16)
    left_low = (left - left_high.astype(jnp.float32)).astype(jnp.bfloat16)
    right_high = right.astype(jnp.bfloat16)
    right_low = (right - right_high.astype(jnp.float32)).astype(jnp.bfloat16)
    both = dot(jnp.concatenate([left_high, left_low], axis=0), right_high)
    return both[:rows] + (both[rows:] + dot(left_high, right_low))


def relax(f, solid):
    pair = [f[i] + f[i + 1] for i in range(1, 19, 2)]
    diff = [f[i] - f[i + 1] for i in range(1, 19, 2)]
    in_xy = pair[3] + pair[4]
    in_xz = pair[5] + pair[6]
    in_yz = pair[7] + pair[8]
    density = (f[0] + pair[0]) + (pair[1] + pair[2]) + (in_xy + in_xz) + in_yz
    flux = (
        diff[0] + (diff[3] + diff[4]) + (diff[5] + diff[6]),
        diff[1] + (diff[3] - diff[4]) + (diff[7] + diff[8]),
        diff[2] + (diff[5] - diff[6]) + (diff[7] - diff[8]),
    )
    inverse = 1.0 / density
    speed = [j * inverse for j in flux]
    third = density * (1.0 / 3.0)
    square = [j * u for j, u in zip(flux, speed)]
    s_xx = pair[0] + in_xy + in_xz - third - square[0]
    s_yy = pair[1] + in_xy + in_yz - third - square[1]
    s_zz = pair[2] + in_xz + in_yz - third - square[2]
    s_xy = pair[3] - pair[4] - flux[0] * speed[1]
    s_xz = pair[5] - pair[6] - flux[0] * speed[2]
    s_yz = pair[7] - pair[8] - flux[1] * speed[2]
    magnitude = (s_xx * s_xx + s_yy * s_yy + s_zz * s_zz) + 2.0 * (
        s_xy * s_xy + s_xz * s_xz + s_yz * s_yz
    )
    root = jnp.sqrt(
        relax_base * relax_base
        + (18.0 * math.sqrt(2.0) * smagorinsky_sq) * jnp.sqrt(magnitude) * inverse
    )
    rate = jnp.where(solid == 1, 0.0, 2.0 / (relax_base + root))
    keep = 1.0 - rate
    base = density - 1.5 * (square[0] + square[1] + square[2])
    by_axis = rate * (1.0 / 18.0)
    by_edge = rate * (1.0 / 36.0)
    triple = [3.0 * j for j in flux]
    out = [keep * f[0] + (rate * (1.0 / 3.0)) * base]
    for i in range(1, 19, 2):
        c = lattice_c[i]
        along = moved = None
        for axis in range(3):
            if c[axis] == 0:
                continue
            if along is None:
                along, moved = speed[axis], triple[axis]
            elif c[axis] > 0:
                along, moved = along + speed[axis], moved + triple[axis]
            else:
                along, moved = along - speed[axis], moved - triple[axis]
        even = base + 1.5 * (moved * along)
        weight = by_axis if i < 7 else by_edge
        out.append(keep * f[i] + weight * (even + moved))
        out.append(keep * f[i + 1] + weight * (even - moved))
    return out


def kernel(
    n,
    frame_hbm,
    f_hbm,
    solid_hbm,
    flags_hbm,
    cells_hbm,
    pod_hbm,
    mri_hbm,
    f_buf,
    inflow_ref,
    frame_ref,
    cells_ref,
    pod_ref,
    mri_ref,
    at_y,
    at_x,
    solid_buf,
    flags_buf,
    r_buf,
    low,
    high,
    part_send,
    part_recv,
    line_send,
    line_recv,
    in_sem,
    mask_sem,
    part_ssem,
    part_rsem,
    line_ssem,
    line_rsem,
    up_ssem,
    up_rsem,
    down_ssem,
    down_rsem,
):
    planes, height, width = solid_buf.shape
    steps = STEPS
    frames = mri_ref.shape[1]
    local = mri_ref.shape[2]
    modes = pod_ref.shape[2]
    rep = LANES // local
    groups = n // rep
    chunk = 16
    rows = slice(PAD, PAD + height)
    me = lax.axis_index("ax")

    barrier = pltpu.get_barrier_semaphore()

    def greet(k, carry):
        pl.semaphore_signal(
            barrier, inc=1, device_id={"ax": lax.rem(me + k, n)}, device_id_type=MESH
        )
        return carry

    lax.fori_loop(1, n, greet, 0)

    loads = []
    for z in range(planes):
        loads.append(pltpu.make_async_copy(f_hbm.at[:, z], f_buf.at[:, z], in_sem.at[z]))
    solid_load = pltpu.make_async_copy(solid_hbm, solid_buf, mask_sem.at[0])
    flags_load = pltpu.make_async_copy(flags_hbm, flags_buf, mask_sem.at[1])
    pod_load = pltpu.make_async_copy(pod_hbm, pod_ref, mask_sem.at[2])
    mri_load = pltpu.make_async_copy(mri_hbm, mri_ref, mask_sem.at[3])
    cells_load = pltpu.make_async_copy(cells_hbm, cells_ref, mask_sem.at[4])
    frame_load = pltpu.make_async_copy(frame_hbm, frame_ref, mask_sem.at[5])
    frame_load.start()
    mri_load.start()
    pod_load.start()
    loads[planes - 1].start()
    solid_load.start()
    for z in range(planes - 2, -1, -1):
        loads[z].start()
    flags_load.start()
    cells_load.start()
    frame_load.wait()
    mri_load.wait()
    pod_load.wait()

    row_at = lax.broadcasted_iota(jnp.int32, (8, local), 0)
    frame_at = lax.broadcasted_iota(jnp.int32, (frames, local), 0)
    partial = jnp.zeros((8, modes), jnp.float32)
    for j in range(3):
        chosen = jnp.zeros((8, local), jnp.float32)
        for s in range(steps):
            frame = lax.rem(frame_ref[0] + s, frames)
            line = jnp.sum(jnp.where(frame_at == frame, mri_ref[j], 0.0), axis=0, keepdims=True)
            chosen = jnp.where(row_at == s, line, chosen)
        partial = partial + split_dot(chosen, pod_ref[j], (((1,), (0,)), ((), ())))
    part_send[...] = partial[:steps]

    def collide(s, z):
        def at(c, carry):
            r0 = pl.multiple_of(c * chunk, chunk)
            here = pl.ds(r0, chunk)
            there = pl.ds(pl.multiple_of(r0 + PAD, 8), chunk)
            f = [f_buf[i, z, here, :] for i in range(19)]
            relaxed = relax(f, solid_buf[z, here, :])
            for i in range(19):
                r_buf[s, slot_of[i], z, there, :] = relaxed[i]
            return carry

        lax.fori_loop(0, height // chunk, at, 0)

    def up_copy(s):
        return pltpu.make_async_remote_copy(
            src_ref=r_buf.at[s, pl.ds(0, CROSS), planes - 1, pl.ds(PAD, height)],
            dst_ref=low.at[s, :, pl.ds(PAD, height)],
            send_sem=up_ssem.at[s],
            recv_sem=up_rsem.at[s],
            device_id={"ax": lax.rem(me + 1, n)},
            device_id_type=MESH,
        )

    def down_copy(s):
        return pltpu.make_async_remote_copy(
            src_ref=r_buf.at[s, pl.ds(CROSS, CROSS), 0, pl.ds(PAD, height)],
            dst_ref=high.at[s, :, pl.ds(PAD, height)],
            send_sem=down_ssem.at[s],
            recv_sem=down_rsem.at[s],
            device_id={"ax": lax.rem(me + n - 1, n)},
            device_id_type=MESH,
        )

    def part_copy(k):
        return pltpu.make_async_remote_copy(
            src_ref=part_send,
            dst_ref=part_recv.at[k - 1],
            send_sem=part_ssem.at[0],
            recv_sem=part_rsem.at[0],
            device_id={"ax": lax.rem(me + k, n)},
            device_id_type=MESH,
        )

    def all_parts():
        return pltpu.make_async_remote_copy(
            src_ref=part_recv,
            dst_ref=part_recv,
            send_sem=part_ssem.at[0],
            recv_sem=part_rsem.at[0],
            device_id={"ax": lax.rem(me + 1, n)},
            device_id_type=MESH,
        )

    def line_copy(source):
        return pltpu.make_async_remote_copy(
            src_ref=line_send,
            dst_ref=line_recv.at[source - 1],
            send_sem=line_ssem.at[0],
            recv_sem=line_rsem.at[0],
            device_id={"ax": 0},
            device_id_type=MESH,
        )

    def send_up(s):
        @pl.when(me < n - 1)
        def _():
            up_copy(s).start()

    def send_down(s):
        @pl.when(me > 0)
        def _():
            down_copy(s).start()

    def stream(s, z, dirs):
        solid = solid_buf[z] == 1
        for i in dirs:
            step_x, step_y, step_z = lattice_c[i]
            own = r_buf[s, slot_of[i], z, rows, :]
            if i == 0:
                f_buf[i, z] = own
                continue
            moved = slice(PAD - step_y, PAD - step_y + height)
            if 0 <= z - step_z < planes:
                source = r_buf[s, slot_of[i], z - step_z, moved, :]
            elif step_z > 0:
                source = low[s, slot_of[i], moved, :]
            else:
                source = high[s, slot_of[i] - CROSS, moved, :]
            if step_x != 0:
                source = pltpu.roll(source, step_x % width, 1)
            bit = 1 << ((i - 1) % 9)
            linked = (flags_buf[(i - 1) // 9, z] & bit) != 0
            back = r_buf[s, slot_of[opposite_of[i]], z, rows, :]
            f_buf[i, z] = jnp.where(solid, own, jnp.where(linked, back, source))

    def all_lines():
        return pltpu.make_async_remote_copy(
            src_ref=line_recv,
            dst_ref=line_recv,
            send_sem=line_ssem.at[0],
            recv_sem=line_rsem.at[0],
            device_id={"ax": lax.rem(me + 1, n)},
            device_id_type=MESH,
        )

    def one_hot():
        cells = cells_ref[...]
        count = cells.shape[1]
        if width & (width - 1) == 0:
            cell_y = lax.shift_right_logical(cells, width.bit_length() - 1)
            cell_x = cells & (width - 1)
        else:
            cell_y = cells // width
            cell_x = cells - cell_y * width
        rows_y = lax.broadcasted_iota(jnp.int32, (height, count), 0) == cell_y
        rows_x = lax.broadcasted_iota(jnp.int32, (width, count), 0) == cell_x
        at_y[...] = jnp.where(rows_y, 1.0, 0.0).astype(jnp.bfloat16)
        at_x[...] = jnp.where(rows_x, 1.0, 0.0).astype(jnp.bfloat16)

    def inlet():
        all_lines().wait_recv()
        own = line_send[...]
        received = [own] + [line_recv[k] for k in range(n - 1)]
        lines = [
            functools.reduce(jnp.add, received[g * rep : (g + 1) * rep]) for g in range(groups)
        ]
        count = at_y.shape[1]
        lit = at_y[...]
        terms = []
        rest = jnp.concatenate(
            [
                jnp.concatenate([v[j] for v in lines], axis=1)
                for j in range(3)
            ]
            + [jnp.zeros((8 - 3 * steps, count), jnp.float32)] * (3 * steps < 8),
            axis=0,
        )
        for _ in range(3):
            head = rest.astype(jnp.bfloat16)
            rest = rest - head.astype(jnp.float32)
            head = head.astype(jnp.float32)
            terms += [
                lit * jnp.broadcast_to(head[r : r + 1], lit.shape).astype(jnp.bfloat16)
                for r in range(3 * steps)
            ]
        found = lax.dot_general(
            jnp.concatenate(terms, axis=0),
            at_x[...],
            (((1,), (1,)), ((), ())),
            preferred_element_type=jnp.float32,
        )
        size = 3 * steps * height
        plane = found[:size] + (found[size : 2 * size] + found[2 * size :])
        for s in range(steps):
            v = [
                inflow_scale * plane[(steps * j + s) * height : (steps * j + s + 1) * height]
                for j in range(3)
            ]
            speed_sq = v[0] * v[0] + v[1] * v[1] + v[2] * v[2]
            for k, i in enumerate(up_dirs):
                along = v[2]
                for axis in range(2):
                    if lattice_c[i][axis] > 0:
                        along = along + v[axis]
                    elif lattice_c[i][axis] < 0:
                        along = along - v[axis]
                low[s, k, rows, :] = lattice_w[i] * (
                    1.0 + 3.0 * along + 4.5 * along * along - 1.5 * speed_sq
                )

    loads[planes - 1].wait()
    solid_load.wait()
    collide(0, planes - 1)
    cells_load.wait()
    pl.semaphore_wait(barrier, n - 1)

    def part_start(k, carry):
        part_copy(k).start()
        return carry

    lax.fori_loop(1, n, part_start, 0)
    send_up(0)
    for z in range(planes - 2, -1, -1):
        loads[z].wait()
        collide(0, z)
    send_down(0)
    flags_load.wait()
    pl.when(me == 0)(one_hot)

    def early(s, z, flat):
        dirs = [
            i
            for i in range(19)
            if (lattice_c[i][2] == 0) == flat and 0 <= z - lattice_c[i][2] < planes
        ]
        stream(s, z, dirs)

    for z in range(planes):
        early(0, z, True)
    for s in range(steps):
        last = s == steps - 1
        for z in range(planes - 1, -1, -1):
            early(s, z, False)
        if s == 0:
            all_parts().wait_recv()
            total = part_send[...] + jnp.sum(part_recv[...], axis=0)
            total = jnp.concatenate([total, jnp.zeros((8 - steps, modes), jnp.float32)], axis=0)
            basis = jnp.concatenate([pod_ref[j] for j in range(3)], axis=0)
            if 3 * local < LANES:
                basis = jnp.concatenate(
                    [basis, jnp.zeros((LANES - 3 * local, modes), jnp.float32)], axis=0
                )
            lines = split_dot(total, basis, (((1,), (1,)), ((), ())))
            lane = lax.broadcasted_iota(jnp.int32, (steps, LANES), 1)
            first = lax.rem(me, rep) * local
            mine = (lane >= first) & (lane < first + local)
            for j in range(3):
                inflow_ref[j] = lines[:steps, j * local : (j + 1) * local]
                turn = lax.rem(first + (LANES - j * local), LANES)
                line_send[j] = jnp.where(mine, pltpu.roll(lines, turn, 1)[:steps], 0.0)

            @pl.when(me > 0)
            def _():
                line_copy(me).start()

        for z in range(planes - 1, -1, -1):
            if z == planes - 1:

                @pl.when(me < n - 1)
                def _():
                    down_copy(s).wait_recv()

                @pl.when(me == n - 1)
                def _():
                    for k in range(CROSS):
                        high[s, k, rows, :] = r_buf[s, CROSS + k, planes - 1, rows, :]

                stream(s, z, down_dirs)
            if z == 0:
                if s == 0:
                    pl.when(me == 0)(inlet)

                @pl.when(me > 0)
                def _():
                    up_copy(s).wait_recv()

                stream(s, z, up_dirs)
            if not last:
                collide(s + 1, z)
                if z == planes - 1:
                    send_up(s + 1)
                if z == 0:
                    send_down(s + 1)
                early(s + 1, z, True)

    all_parts().wait_send()

    @pl.when(me > 0)
    def _():
        line_copy(me).wait_send()
        for s in range(steps):
            down_copy(s).wait_send()

    @pl.when(me < n - 1)
    def _():
        for s in range(steps):
            up_copy(s).wait_send()


def finish(f_ref, inflow_ref, out_hbm, inflow_hbm, sem):
    copies = [
        pltpu.make_async_copy(f_ref, out_hbm, sem.at[0]),
        pltpu.make_async_copy(inflow_ref, inflow_hbm, sem.at[1]),
    ]
    for copy in copies:
        copy.start()
    for copy in copies:
        copy.wait()


def body(n, populations, solid_mask, link_flags, inlet_cells, pod_basis, mri_frames, frame_index):
    planes, height, width = solid_mask.shape
    modes, _, local = pod_basis.shape
    if planes < 2 or LANES % local or n % (LANES // local) or width != LANES or height % 16:
        raise ValueError("sizes")
    dma = pltpu.SemaphoreType.DMA
    f32 = jnp.float32
    wide = pltpu.CompilerParams(vmem_limit_bytes=32 * 1024 * 1024)
    on_chip = pl.BlockSpec(memory_space=pltpu.VMEM)
    anywhere = pl.BlockSpec(memory_space=pl.ANY)
    advanced, inflow = pl.pallas_call(
        functools.partial(kernel, n),
        name="lattice",
        out_shape=(
            pltpu.VMEM(populations.shape, f32),
            pltpu.VMEM((3, STEPS, local), f32),
        ),
        in_specs=[pl.BlockSpec(memory_space=pltpu.HBM)] * 7,
        out_specs=(on_chip, on_chip),
        scratch_shapes=[
            pltpu.SMEM((1,), jnp.int32),
            pltpu.VMEM((1, inlet_cells.shape[0]), jnp.int32),
            pltpu.VMEM((3, local, modes), f32),
            pltpu.VMEM((3, mri_frames.shape[0], local), f32),
            pltpu.VMEM((height, inlet_cells.shape[0]), jnp.bfloat16),
            pltpu.VMEM((width, inlet_cells.shape[0]), jnp.bfloat16),
            pltpu.VMEM((planes, height, width), jnp.int32),
            pltpu.VMEM((2, planes, height, width), jnp.int32),
            pltpu.VMEM((STEPS, 19, planes, height + 2 * PAD, width), f32),
            pltpu.VMEM((STEPS, CROSS, height + 2 * PAD, width), f32),
            pltpu.VMEM((STEPS, CROSS, height + 2 * PAD, width), f32),
            pltpu.VMEM((STEPS, modes), f32),
            pltpu.VMEM((n - 1, STEPS, modes), f32),
            pltpu.VMEM((3, STEPS, LANES), f32),
            pltpu.VMEM((n - 1, 3, STEPS, LANES), f32),
            dma((planes,)),
            dma((6,)),
            dma((1,)),
            dma((1,)),
            dma((1,)),
            dma((1,)),
            dma((STEPS,)),
            dma((STEPS,)),
            dma((STEPS,)),
            dma((STEPS,)),
        ],
        compiler_params=pltpu.CompilerParams(
            collective_id=0, has_side_effects=True, vmem_limit_bytes=32 * 1024 * 1024
        ),
    )(
        frame_index,
        populations,
        solid_mask,
        link_flags,
        inlet_cells.reshape(1, -1),
        jnp.transpose(pod_basis, (1, 2, 0)),
        jnp.transpose(mri_frames, (1, 0, 2)),
    )
    advanced, inflow = pl.pallas_call(
        finish,
        name="finish",
        out_shape=(
            jax.ShapeDtypeStruct(populations.shape, f32),
            jax.ShapeDtypeStruct((3, STEPS, local), f32),
        ),
        in_specs=[on_chip, on_chip],
        out_specs=(anywhere, anywhere),
        scratch_shapes=[dma((2,))],
        compiler_params=wide,
    )(advanced, inflow)
    return advanced, jnp.transpose(inflow, (1, 0, 2))


def solution(mesh):
    in_specs = (
        P(None, "ax", "case", None),
        P("ax", "case", None),
        P(None, "ax", "case", None),
        P("case"),
        P(None, None, "ax"),
        P(None, "case", "ax"),
        P(),
    )
    out_specs = (P(None, "ax", "case", None), P(None, "case", "ax"))
    return jax.shard_map(
        functools.partial(body, mesh.shape["ax"]),
        mesh=mesh,
        in_specs=in_specs,
        out_specs=out_specs,
        check_vma=False,
    )
```

```python
import functools
import math

import jax
import jax.numpy as jnp
from jax import lax
from jax.experimental import pallas as pl
from jax.experimental.pallas import tpu as pltpu
from jax.sharding import PartitionSpec as P

STEPS = 2
MESH = pl.DeviceIdType.MESH
PAD = 8
LANES = 128

lattice_c = (
    (0, 0, 0),
    (1, 0, 0),
    (-1, 0, 0),
    (0, 1, 0),
    (0, -1, 0),
    (0, 0, 1),
    (0, 0, -1),
    (1, 1, 0),
    (-1, -1, 0),
    (1, -1, 0),
    (-1, 1, 0),
    (1, 0, 1),
    (-1, 0, -1),
    (1, 0, -1),
    (-1, 0, 1),
    (0, 1, 1),
    (0, -1, -1),
    (0, 1, -1),
    (0, -1, 1),
)
lattice_w = (1.0 / 3.0,) + (1.0 / 18.0,) * 6 + (1.0 / 36.0,) * 12
opposite_of = (0, 2, 1, 4, 3, 6, 5, 8, 7, 10, 9, 12, 11, 14, 13, 16, 15, 18, 17)
relax_base = 0.52
smagorinsky_sq = 0.04
inflow_scale = 0.05

up_dirs = tuple(i for i in range(19) if lattice_c[i][2] == 1)
down_dirs = tuple(i for i in range(19) if lattice_c[i][2] == -1)
flat_dirs = tuple(i for i in range(19) if lattice_c[i][2] == 0)
slot_of = {d: k for k, d in enumerate(up_dirs + down_dirs + flat_dirs)}
CROSS = len(up_dirs)


def split_dot(left, right, dims):
    dot = functools.partial(
        lax.dot_general, dimension_numbers=dims, preferred_element_type=jnp.float32
    )
    rows = left.shape[0]
    left_high = left.astype(jnp.bfloat16)
    left_low = (left - left_high.astype(jnp.float32)).astype(jnp.bfloat16)
    right_high = right.astype(jnp.bfloat16)
    right_low = (right - right_high.astype(jnp.float32)).astype(jnp.bfloat16)
    both = dot(jnp.concatenate([left_high, left_low], axis=0), right_high)
    return both[:rows] + (both[rows:] + dot(left_high, right_low))


def relax(f, solid):
    pair = [f[i] + f[i + 1] for i in range(1, 19, 2)]
    diff = [f[i] - f[i + 1] for i in range(1, 19, 2)]
    in_xy = pair[3] + pair[4]
    in_xz = pair[5] + pair[6]
    in_yz = pair[7] + pair[8]
    density = (f[0] + pair[0]) + (pair[1] + pair[2]) + (in_xy + in_xz) + in_yz
    flux = (
        diff[0] + (diff[3] + diff[4]) + (diff[5] + diff[6]),
        diff[1] + (diff[3] - diff[4]) + (diff[7] + diff[8]),
        diff[2] + (diff[5] - diff[6]) + (diff[7] - diff[8]),
    )
    inverse = 1.0 / density
    speed = [j * inverse for j in flux]
    third = density * (1.0 / 3.0)
    square = [j * u for j, u in zip(flux, speed)]
    s_xx = pair[0] + in_xy + in_xz - third - square[0]
    s_yy = pair[1] + in_xy + in_yz - third - square[1]
    s_zz = pair[2] + in_xz + in_yz - third - square[2]
    s_xy = pair[3] - pair[4] - flux[0] * speed[1]
    s_xz = pair[5] - pair[6] - flux[0] * speed[2]
    s_yz = pair[7] - pair[8] - flux[1] * speed[2]
    magnitude = (s_xx * s_xx + s_yy * s_yy + s_zz * s_zz) + 2.0 * (
        s_xy * s_xy + s_xz * s_xz + s_yz * s_yz
    )
    root = jnp.sqrt(
        relax_base * relax_base
        + (18.0 * math.sqrt(2.0) * smagorinsky_sq) * jnp.sqrt(magnitude) * inverse
    )
    rate = jnp.where(solid == 1, 0.0, 2.0 / (relax_base + root))
    keep = 1.0 - rate
    base = density - 1.5 * (square[0] + square[1] + square[2])
    by_axis = rate * (1.0 / 18.0)
    by_edge = rate * (1.0 / 36.0)
    triple = [3.0 * j for j in flux]
    out = [keep * f[0] + (rate * (1.0 / 3.0)) * base]
    for i in range(1, 19, 2):
        c = lattice_c[i]
        along = moved = None
        for axis in range(3):
            if c[axis] == 0:
                continue
            if along is None:
                along, moved = speed[axis], triple[axis]
            elif c[axis] > 0:
                along, moved = along + speed[axis], moved + triple[axis]
            else:
                along, moved = along - speed[axis], moved - triple[axis]
        even = base + 1.5 * (moved * along)
        weight = by_axis if i < 7 else by_edge
        out.append(keep * f[i] + weight * (even + moved))
        out.append(keep * f[i + 1] + weight * (even - moved))
    return out


def kernel(
    n,
    frame_ref,
    f_hbm,
    solid_hbm,
    flags_hbm,
    cells_hbm,
    pod_hbm,
    mri_hbm,
    f_buf,
    inflow_ref,
    cells_ref,
    pod_ref,
    mri_ref,
    at_y,
    at_x,
    solid_buf,
    flags_buf,
    r_buf,
    low,
    high,
    part_send,
    part_recv,
    line_send,
    line_recv,
    in_sem,
    mask_sem,
    part_ssem,
    part_rsem,
    line_ssem,
    line_rsem,
    up_ssem,
    up_rsem,
    down_ssem,
    down_rsem,
):
    planes, height, width = solid_buf.shape
    steps = STEPS
    frames = mri_ref.shape[1]
    local = mri_ref.shape[2]
    modes = pod_ref.shape[2]
    rep = LANES // local
    groups = n // rep
    chunk = 16
    rows = slice(PAD, PAD + height)
    me = lax.axis_index("ax")

    barrier = pltpu.get_barrier_semaphore()

    def greet(k, carry):
        pl.semaphore_signal(
            barrier, inc=1, device_id={"ax": lax.rem(me + k, n)}, device_id_type=MESH
        )
        return carry

    lax.fori_loop(1, n, greet, 0)

    loads = []
    for z in range(planes):
        loads.append(pltpu.make_async_copy(f_hbm.at[:, z], f_buf.at[:, z], in_sem.at[z]))
    solid_load = pltpu.make_async_copy(solid_hbm, solid_buf, mask_sem.at[0])
    flags_load = pltpu.make_async_copy(flags_hbm, flags_buf, mask_sem.at[1])
    pod_load = pltpu.make_async_copy(pod_hbm, pod_ref, mask_sem.at[2])
    mri_load = pltpu.make_async_copy(mri_hbm, mri_ref, mask_sem.at[3])
    cells_load = pltpu.make_async_copy(cells_hbm, cells_ref, mask_sem.at[4])
    mri_load.start()
    pod_load.start()
    loads[planes - 1].start()
    solid_load.start()
    for z in range(planes - 2, -1, -1):
        loads[z].start()
    flags_load.start()
    cells_load.start()
    mri_load.wait()
    pod_load.wait()

    row_at = lax.broadcasted_iota(jnp.int32, (8, local), 0)
    frame_at = lax.broadcasted_iota(jnp.int32, (frames, local), 0)
    partial = jnp.zeros((8, modes), jnp.float32)
    for j in range(3):
        chosen = jnp.zeros((8, local), jnp.float32)
        for s in range(steps):
            frame = lax.rem(frame_ref[0] + s, frames)
            line = jnp.sum(jnp.where(frame_at == frame, mri_ref[j], 0.0), axis=0, keepdims=True)
            chosen = jnp.where(row_at == s, line, chosen)
        partial = partial + split_dot(chosen, pod_ref[j], (((1,), (0,)), ((), ())))
    part_send[...] = partial[:steps]

    def collide(s, z):
        def at(c, carry):
            r0 = pl.multiple_of(c * chunk, chunk)
            here = pl.ds(r0, chunk)
            there = pl.ds(pl.multiple_of(r0 + PAD, 8), chunk)
            f = [f_buf[i, z, here, :] for i in range(19)]
            relaxed = relax(f, solid_buf[z, here, :])
            for i in range(19):
                r_buf[s, slot_of[i], z, there, :] = relaxed[i]
            return carry

        lax.fori_loop(0, height // chunk, at, 0)

    def up_copy(s):
        return pltpu.make_async_remote_copy(
            src_ref=r_buf.at[s, pl.ds(0, CROSS), planes - 1, pl.ds(PAD, height)],
            dst_ref=low.at[s, :, pl.ds(PAD, height)],
            send_sem=up_ssem.at[s],
            recv_sem=up_rsem.at[s],
            device_id={"ax": lax.rem(me + 1, n)},
            device_id_type=MESH,
        )

    def down_copy(s):
        return pltpu.make_async_remote_copy(
            src_ref=r_buf.at[s, pl.ds(CROSS, CROSS), 0, pl.ds(PAD, height)],
            dst_ref=high.at[s, :, pl.ds(PAD, height)],
            send_sem=down_ssem.at[s],
            recv_sem=down_rsem.at[s],
            device_id={"ax": lax.rem(me + n - 1, n)},
            device_id_type=MESH,
        )

    def part_copy(k):
        return pltpu.make_async_remote_copy(
            src_ref=part_send,
            dst_ref=part_recv.at[k - 1],
            send_sem=part_ssem.at[0],
            recv_sem=part_rsem.at[0],
            device_id={"ax": lax.rem(me + k, n)},
            device_id_type=MESH,
        )

    def all_parts():
        return pltpu.make_async_remote_copy(
            src_ref=part_recv,
            dst_ref=part_recv,
            send_sem=part_ssem.at[0],
            recv_sem=part_rsem.at[0],
            device_id={"ax": lax.rem(me + 1, n)},
            device_id_type=MESH,
        )

    def line_copy(source):
        return pltpu.make_async_remote_copy(
            src_ref=line_send,
            dst_ref=line_recv.at[source - 1],
            send_sem=line_ssem.at[0],
            recv_sem=line_rsem.at[0],
            device_id={"ax": 0},
            device_id_type=MESH,
        )

    def send_up(s):
        @pl.when(me < n - 1)
        def _():
            up_copy(s).start()

    def send_down(s):
        @pl.when(me > 0)
        def _():
            down_copy(s).start()

    def stream(s, z, dirs):
        solid = solid_buf[z] == 1
        for i in dirs:
            step_x, step_y, step_z = lattice_c[i]
            own = r_buf[s, slot_of[i], z, rows, :]
            if i == 0:
                f_buf[i, z] = own
                continue
            moved = slice(PAD - step_y, PAD - step_y + height)
            if 0 <= z - step_z < planes:
                source = r_buf[s, slot_of[i], z - step_z, moved, :]
            elif step_z > 0:
                source = low[s, slot_of[i], moved, :]
            else:
                source = high[s, slot_of[i] - CROSS, moved, :]
            if step_x != 0:
                source = pltpu.roll(source, step_x % width, 1)
            bit = 1 << ((i - 1) % 9)
            linked = (flags_buf[(i - 1) // 9, z] & bit) != 0
            back = r_buf[s, slot_of[opposite_of[i]], z, rows, :]
            f_buf[i, z] = jnp.where(solid, own, jnp.where(linked, back, source))

    def all_lines():
        return pltpu.make_async_remote_copy(
            src_ref=line_recv,
            dst_ref=line_recv,
            send_sem=line_ssem.at[0],
            recv_sem=line_rsem.at[0],
            device_id={"ax": lax.rem(me + 1, n)},
            device_id_type=MESH,
        )

    def one_hot():
        cells = cells_ref[...]
        count = cells.shape[1]
        if width & (width - 1) == 0:
            cell_y = lax.shift_right_logical(cells, width.bit_length() - 1)
            cell_x = cells & (width - 1)
        else:
            cell_y = cells // width
            cell_x = cells - cell_y * width
        rows_y = lax.broadcasted_iota(jnp.int32, (height, count), 0) == cell_y
        rows_x = lax.broadcasted_iota(jnp.int32, (width, count), 0) == cell_x
        at_y[...] = jnp.where(rows_y, 1.0, 0.0).astype(jnp.bfloat16)
        at_x[...] = jnp.where(rows_x, 1.0, 0.0).astype(jnp.bfloat16)

    def inlet():
        all_lines().wait_recv()
        own = line_send[...]
        received = [own] + [line_recv[k] for k in range(n - 1)]
        lines = [
            functools.reduce(jnp.add, received[g * rep : (g + 1) * rep]) for g in range(groups)
        ]
        count = at_y.shape[1]
        lit = at_y[...]
        terms = []
        rest = jnp.concatenate(
            [
                jnp.concatenate([v[j] for v in lines], axis=1)
                for j in range(3)
            ]
            + [jnp.zeros((8 - 3 * steps, count), jnp.float32)] * (3 * steps < 8),
            axis=0,
        )
        for _ in range(3):
            head = rest.astype(jnp.bfloat16)
            rest = rest - head.astype(jnp.float32)
            head = head.astype(jnp.float32)
            terms += [
                lit * jnp.broadcast_to(head[r : r + 1], lit.shape).astype(jnp.bfloat16)
                for r in range(3 * steps)
            ]
        found = lax.dot_general(
            jnp.concatenate(terms, axis=0),
            at_x[...],
            (((1,), (1,)), ((), ())),
            preferred_element_type=jnp.float32,
        )
        size = 3 * steps * height
        plane = found[:size] + (found[size : 2 * size] + found[2 * size :])
        for s in range(steps):
            v = [
                inflow_scale * plane[(steps * j + s) * height : (steps * j + s + 1) * height]
                for j in range(3)
            ]
            speed_sq = v[0] * v[0] + v[1] * v[1] + v[2] * v[2]
            for k, i in enumerate(up_dirs):
                along = v[2]
                for axis in range(2):
                    if lattice_c[i][axis] > 0:
                        along = along + v[axis]
                    elif lattice_c[i][axis] < 0:
                        along = along - v[axis]
                low[s, k, rows, :] = lattice_w[i] * (
                    1.0 + 3.0 * along + 4.5 * along * along - 1.5 * speed_sq
                )

    loads[planes - 1].wait()
    solid_load.wait()
    collide(0, planes - 1)
    cells_load.wait()
    pl.semaphore_wait(barrier, n - 1)

    def part_start(k, carry):
        part_copy(k).start()
        return carry

    lax.fori_loop(1, n, part_start, 0)
    send_up(0)
    for z in range(planes - 2, -1, -1):
        loads[z].wait()
        collide(0, z)
    send_down(0)
    flags_load.wait()
    pl.when(me == 0)(one_hot)

    def early(s, z, flat):
        dirs = [
            i
            for i in range(19)
            if (lattice_c[i][2] == 0) == flat and 0 <= z - lattice_c[i][2] < planes
        ]
        stream(s, z, dirs)

    for z in range(planes):
        early(0, z, True)
    for s in range(steps):
        last = s == steps - 1
        for z in range(planes - 1, -1, -1):
            early(s, z, False)
        if s == 0:
            all_parts().wait_recv()
            total = part_send[...] + jnp.sum(part_recv[...], axis=0)
            total = jnp.concatenate([total, jnp.zeros((8 - steps, modes), jnp.float32)], axis=0)
            basis = jnp.concatenate([pod_ref[j] for j in range(3)], axis=0)
            if 3 * local < LANES:
                basis = jnp.concatenate(
                    [basis, jnp.zeros((LANES - 3 * local, modes), jnp.float32)], axis=0
                )
            lines = split_dot(total, basis, (((1,), (1,)), ((), ())))
            lane = lax.broadcasted_iota(jnp.int32, (steps, LANES), 1)
            first = lax.rem(me, rep) * local
            mine = (lane >= first) & (lane < first + local)
            for j in range(3):
                inflow_ref[j] = lines[:steps, j * local : (j + 1) * local]
                turn = lax.rem(first + (LANES - j * local), LANES)
                line_send[j] = jnp.where(mine, pltpu.roll(lines, turn, 1)[:steps], 0.0)

            @pl.when(me > 0)
            def _():
                line_copy(me).start()

        for z in range(planes - 1, -1, -1):
            if z == planes - 1:

                @pl.when(me < n - 1)
                def _():
                    down_copy(s).wait_recv()

                @pl.when(me == n - 1)
                def _():
                    for k in range(CROSS):
                        high[s, k, rows, :] = r_buf[s, CROSS + k, planes - 1, rows, :]

                stream(s, z, down_dirs)
            if z == 0:
                if s == 0:
                    pl.when(me == 0)(inlet)

                @pl.when(me > 0)
                def _():
                    up_copy(s).wait_recv()

                stream(s, z, up_dirs)
            if not last:
                collide(s + 1, z)
                if z == planes - 1:
                    send_up(s + 1)
                if z == 0:
                    send_down(s + 1)
                early(s + 1, z, True)

    all_parts().wait_send()

    @pl.when(me > 0)
    def _():
        line_copy(me).wait_send()
        for s in range(steps):
            down_copy(s).wait_send()

    @pl.when(me < n - 1)
    def _():
        for s in range(steps):
            up_copy(s).wait_send()


def finish(f_ref, inflow_ref, out_hbm, inflow_hbm, sem):
    copies = [
        pltpu.make_async_copy(f_ref, out_hbm, sem.at[0]),
        pltpu.make_async_copy(inflow_ref, inflow_hbm, sem.at[1]),
    ]
    for copy in copies:
        copy.start()
    for copy in copies:
        copy.wait()


def body(n, populations, solid_mask, link_flags, inlet_cells, pod_basis, mri_frames, frame_index):
    planes, height, width = solid_mask.shape
    modes, _, local = pod_basis.shape
    if planes < 2 or LANES % local or n % (LANES // local) or width != LANES or height % 16:
        raise ValueError("sizes")
    dma = pltpu.SemaphoreType.DMA
    f32 = jnp.float32
    wide = pltpu.CompilerParams(vmem_limit_bytes=32 * 1024 * 1024)
    on_chip = pl.BlockSpec(memory_space=pltpu.VMEM)
    in_hbm = pl.BlockSpec(memory_space=pltpu.HBM)
    anywhere = pl.BlockSpec(memory_space=pl.ANY)
    advanced, inflow = pl.pallas_call(
        functools.partial(kernel, n),
        name="lattice",
        out_shape=(
            pltpu.VMEM(populations.shape, f32),
            pltpu.VMEM((3, STEPS, local), f32),
        ),
        in_specs=[pl.BlockSpec(memory_space=pltpu.SMEM)] + [in_hbm] * 6,
        out_specs=(on_chip, on_chip),
        scratch_shapes=[
            pltpu.VMEM((1, inlet_cells.shape[0]), jnp.int32),
            pltpu.VMEM((3, local, modes), f32),
            pltpu.VMEM((3, mri_frames.shape[0], local), f32),
            pltpu.VMEM((height, inlet_cells.shape[0]), jnp.bfloat16),
            pltpu.VMEM((width, inlet_cells.shape[0]), jnp.bfloat16),
            pltpu.VMEM((planes, height, width), jnp.int32),
            pltpu.VMEM((2, planes, height, width), jnp.int32),
            pltpu.VMEM((STEPS, 19, planes, height + 2 * PAD, width), f32),
            pltpu.VMEM((STEPS, CROSS, height + 2 * PAD, width), f32),
            pltpu.VMEM((STEPS, CROSS, height + 2 * PAD, width), f32),
            pltpu.VMEM((STEPS, modes), f32),
            pltpu.VMEM((n - 1, STEPS, modes), f32),
            pltpu.VMEM((3, STEPS, LANES), f32),
            pltpu.VMEM((n - 1, 3, STEPS, LANES), f32),
            dma((planes,)),
            dma((5,)),
            dma((1,)),
            dma((1,)),
            dma((1,)),
            dma((1,)),
            dma((STEPS,)),
            dma((STEPS,)),
            dma((STEPS,)),
            dma((STEPS,)),
        ],
        compiler_params=pltpu.CompilerParams(
            collective_id=0, has_side_effects=True, vmem_limit_bytes=32 * 1024 * 1024
        ),
    )(
        frame_index,
        *(
            pltpu.with_memory_space_constraint(operand, pltpu.HBM)
            for operand in (
                populations,
                solid_mask,
                link_flags,
                inlet_cells.reshape(1, -1),
                jnp.transpose(pod_basis, (1, 2, 0)),
                jnp.transpose(mri_frames, (1, 0, 2)),
            )
        )
    )
    advanced, inflow = pl.pallas_call(
        finish,
        name="finish",
        out_shape=(
            jax.ShapeDtypeStruct(populations.shape, f32),
            jax.ShapeDtypeStruct((3, STEPS, local), f32),
        ),
        in_specs=[on_chip, on_chip],
        out_specs=(anywhere, anywhere),
        scratch_shapes=[dma((2,))],
        compiler_params=wide,
    )(advanced, inflow)
    return advanced, jnp.transpose(inflow, (1, 0, 2))


def solution(mesh):
    in_specs = (
        P(None, "ax", "case", None),
        P("ax", "case", None),
        P(None, "ax", "case", None),
        P("case"),
        P(None, None, "ax"),
        P(None, "case", "ax"),
        P(),
    )
    out_specs = (P(None, "ax", "case", None), P(None, "case", "ax"))
    return jax.shard_map(
        functools.partial(body, mesh.shape["ax"]),
        mesh=mesh,
        in_specs=in_specs,
        out_specs=out_specs,
        check_vma=False,
    )
```

```python
import functools
import math

import jax
import jax.numpy as jnp
from jax import lax
from jax.experimental import pallas as pl
from jax.experimental.pallas import tpu as pltpu
from jax.sharding import PartitionSpec as P

STEPS = 2
MESH = pl.DeviceIdType.MESH
PAD = 8
LANES = 128

lattice_c = (
    (0, 0, 0),
    (1, 0, 0),
    (-1, 0, 0),
    (0, 1, 0),
    (0, -1, 0),
    (0, 0, 1),
    (0, 0, -1),
    (1, 1, 0),
    (-1, -1, 0),
    (1, -1, 0),
    (-1, 1, 0),
    (1, 0, 1),
    (-1, 0, -1),
    (1, 0, -1),
    (-1, 0, 1),
    (0, 1, 1),
    (0, -1, -1),
    (0, 1, -1),
    (0, -1, 1),
)
lattice_w = (1.0 / 3.0,) + (1.0 / 18.0,) * 6 + (1.0 / 36.0,) * 12
opposite_of = (0, 2, 1, 4, 3, 6, 5, 8, 7, 10, 9, 12, 11, 14, 13, 16, 15, 18, 17)
relax_base = 0.52
smagorinsky_sq = 0.04
inflow_scale = 0.05

up_dirs = tuple(i for i in range(19) if lattice_c[i][2] == 1)
down_dirs = tuple(i for i in range(19) if lattice_c[i][2] == -1)
flat_dirs = tuple(i for i in range(19) if lattice_c[i][2] == 0)
slot_of = {d: k for k, d in enumerate(up_dirs + down_dirs + flat_dirs)}
CROSS = len(up_dirs)


def split_dot(left, right, dims):
    dot = functools.partial(
        lax.dot_general, dimension_numbers=dims, preferred_element_type=jnp.float32
    )
    rows = left.shape[0]
    left_high = left.astype(jnp.bfloat16)
    left_low = (left - left_high.astype(jnp.float32)).astype(jnp.bfloat16)
    right_high = right.astype(jnp.bfloat16)
    right_low = (right - right_high.astype(jnp.float32)).astype(jnp.bfloat16)
    both = dot(jnp.concatenate([left_high, left_low], axis=0), right_high)
    return both[:rows] + (both[rows:] + dot(left_high, right_low))


def relax(f, solid):
    pair = [f[i] + f[i + 1] for i in range(1, 19, 2)]
    diff = [f[i] - f[i + 1] for i in range(1, 19, 2)]
    in_xy = pair[3] + pair[4]
    in_xz = pair[5] + pair[6]
    in_yz = pair[7] + pair[8]
    density = (f[0] + pair[0]) + (pair[1] + pair[2]) + (in_xy + in_xz) + in_yz
    flux = (
        diff[0] + (diff[3] + diff[4]) + (diff[5] + diff[6]),
        diff[1] + (diff[3] - diff[4]) + (diff[7] + diff[8]),
        diff[2] + (diff[5] - diff[6]) + (diff[7] - diff[8]),
    )
    inverse = 1.0 / density
    speed = [j * inverse for j in flux]
    third = density * (1.0 / 3.0)
    square = [j * u for j, u in zip(flux, speed)]
    s_xx = pair[0] + in_xy + in_xz - third - square[0]
    s_yy = pair[1] + in_xy + in_yz - third - square[1]
    s_zz = pair[2] + in_xz + in_yz - third - square[2]
    s_xy = pair[3] - pair[4] - flux[0] * speed[1]
    s_xz = pair[5] - pair[6] - flux[0] * speed[2]
    s_yz = pair[7] - pair[8] - flux[1] * speed[2]
    magnitude = (s_xx * s_xx + s_yy * s_yy + s_zz * s_zz) + 2.0 * (
        s_xy * s_xy + s_xz * s_xz + s_yz * s_yz
    )
    root = jnp.sqrt(
        relax_base * relax_base
        + (18.0 * math.sqrt(2.0) * smagorinsky_sq) * jnp.sqrt(magnitude) * inverse
    )
    rate = jnp.where(solid == 1, 0.0, 2.0 / (relax_base + root))
    keep = 1.0 - rate
    base = density - 1.5 * (square[0] + square[1] + square[2])
    by_axis = rate * (1.0 / 18.0)
    by_edge = rate * (1.0 / 36.0)
    triple = [3.0 * j for j in flux]
    out = [keep * f[0] + (rate * (1.0 / 3.0)) * base]
    for i in range(1, 19, 2):
        c = lattice_c[i]
        along = moved = None
        for axis in range(3):
            if c[axis] == 0:
                continue
            if along is None:
                along, moved = speed[axis], triple[axis]
            elif c[axis] > 0:
                along, moved = along + speed[axis], moved + triple[axis]
            else:
                along, moved = along - speed[axis], moved - triple[axis]
        even = base + 1.5 * (moved * along)
        weight = by_axis if i < 7 else by_edge
        out.append(keep * f[i] + weight * (even + moved))
        out.append(keep * f[i + 1] + weight * (even - moved))
    return out


def kernel(
    n,
    frame_ref,
    f_hbm,
    solid_hbm,
    flags_hbm,
    cells_hbm,
    pod_hbm,
    mri_hbm,
    f_buf,
    inflow_ref,
    cells_ref,
    pod_ref,
    mri_ref,
    at_y,
    at_x,
    solid_buf,
    flags_buf,
    r_buf,
    low,
    high,
    part_send,
    part_recv,
    line_send,
    line_recv,
    in_sem,
    mask_sem,
    part_ssem,
    part_rsem,
    line_ssem,
    line_rsem,
    up_ssem,
    up_rsem,
    down_ssem,
    down_rsem,
):
    planes, height, width = solid_buf.shape
    steps = STEPS
    frames = mri_ref.shape[1]
    local = mri_ref.shape[2]
    modes = pod_ref.shape[2]
    rep = LANES // local
    groups = n // rep
    chunk = 16
    rows = slice(PAD, PAD + height)
    me = lax.axis_index("ax")

    barrier = pltpu.get_barrier_semaphore()

    def greet(k, carry):
        pl.semaphore_signal(
            barrier, inc=1, device_id={"ax": lax.rem(me + k, n)}, device_id_type=MESH
        )
        return carry

    lax.fori_loop(1, n, greet, 0)

    loads = []
    for z in range(planes):
        loads.append(pltpu.make_async_copy(f_hbm.at[:, z], f_buf.at[:, z], in_sem.at[z]))
    solid_load = pltpu.make_async_copy(solid_hbm, solid_buf, mask_sem.at[0])
    flags_load = pltpu.make_async_copy(flags_hbm, flags_buf, mask_sem.at[1])
    pod_load = pltpu.make_async_copy(pod_hbm, pod_ref, mask_sem.at[2])
    mri_load = pltpu.make_async_copy(mri_hbm, mri_ref, mask_sem.at[3])
    cells_load = pltpu.make_async_copy(cells_hbm, cells_ref, mask_sem.at[4])
    mri_load.start()
    pod_load.start()
    loads[planes - 1].start()
    solid_load.start()
    for z in range(planes - 2, -1, -1):
        loads[z].start()
    flags_load.start()
    cells_load.start()
    mri_load.wait()
    pod_load.wait()

    row_at = lax.broadcasted_iota(jnp.int32, (8, local), 0)
    frame_at = lax.broadcasted_iota(jnp.int32, (frames, local), 0)
    partial = jnp.zeros((8, modes), jnp.float32)
    for j in range(3):
        chosen = jnp.zeros((8, local), jnp.float32)
        for s in range(steps):
            frame = lax.rem(frame_ref[0] + s, frames)
            line = jnp.sum(jnp.where(frame_at == frame, mri_ref[j], 0.0), axis=0, keepdims=True)
            chosen = jnp.where(row_at == s, line, chosen)
        partial = partial + split_dot(chosen, pod_ref[j], (((1,), (0,)), ((), ())))
    part_send[...] = partial[:steps]

    def collide(s, z):
        def at(c, carry):
            r0 = pl.multiple_of(c * chunk, chunk)
            here = pl.ds(r0, chunk)
            there = pl.ds(pl.multiple_of(r0 + PAD, 8), chunk)
            f = [f_buf[i, z, here, :] for i in range(19)]
            relaxed = relax(f, solid_buf[z, here, :])
            for i in range(19):
                r_buf[s, slot_of[i], z, there, :] = relaxed[i]
            return carry

        lax.fori_loop(0, height // chunk, at, 0)

    def up_copy(s):
        return pltpu.make_async_remote_copy(
            src_ref=r_buf.at[s, pl.ds(0, CROSS), planes - 1, pl.ds(PAD, height)],
            dst_ref=low.at[s, :, pl.ds(PAD, height)],
            send_sem=up_ssem.at[s],
            recv_sem=up_rsem.at[s],
            device_id={"ax": lax.rem(me + 1, n)},
            device_id_type=MESH,
        )

    def down_copy(s):
        return pltpu.make_async_remote_copy(
            src_ref=r_buf.at[s, pl.ds(CROSS, CROSS), 0, pl.ds(PAD, height)],
            dst_ref=high.at[s, :, pl.ds(PAD, height)],
            send_sem=down_ssem.at[s],
            recv_sem=down_rsem.at[s],
            device_id={"ax": lax.rem(me + n - 1, n)},
            device_id_type=MESH,
        )

    def part_copy(k):
        return pltpu.make_async_remote_copy(
            src_ref=part_send,
            dst_ref=part_recv.at[k - 1],
            send_sem=part_ssem.at[0],
            recv_sem=part_rsem.at[0],
            device_id={"ax": lax.rem(me + k, n)},
            device_id_type=MESH,
        )

    def all_parts():
        return pltpu.make_async_remote_copy(
            src_ref=part_recv,
            dst_ref=part_recv,
            send_sem=part_ssem.at[0],
            recv_sem=part_rsem.at[0],
            device_id={"ax": lax.rem(me + 1, n)},
            device_id_type=MESH,
        )

    def line_copy(source):
        return pltpu.make_async_remote_copy(
            src_ref=line_send,
            dst_ref=line_recv.at[source - 1],
            send_sem=line_ssem.at[0],
            recv_sem=line_rsem.at[0],
            device_id={"ax": 0},
            device_id_type=MESH,
        )

    def send_up(s):
        @pl.when(me < n - 1)
        def _():
            up_copy(s).start()

    def send_down(s):
        @pl.when(me > 0)
        def _():
            down_copy(s).start()

    def stream(s, z, dirs):
        solid = solid_buf[z] == 1
        for i in dirs:
            step_x, step_y, step_z = lattice_c[i]
            own = r_buf[s, slot_of[i], z, rows, :]
            if i == 0:
                f_buf[i, z] = own
                continue
            moved = slice(PAD - step_y, PAD - step_y + height)
            if 0 <= z - step_z < planes:
                source = r_buf[s, slot_of[i], z - step_z, moved, :]
            elif step_z > 0:
                source = low[s, slot_of[i], moved, :]
            else:
                source = high[s, slot_of[i] - CROSS, moved, :]
            if step_x != 0:
                source = pltpu.roll(source, step_x % width, 1)
            bit = 1 << ((i - 1) % 9)
            linked = (flags_buf[(i - 1) // 9, z] & bit) != 0
            back = r_buf[s, slot_of[opposite_of[i]], z, rows, :]
            f_buf[i, z] = jnp.where(solid, own, jnp.where(linked, back, source))

    def all_lines():
        return pltpu.make_async_remote_copy(
            src_ref=line_recv,
            dst_ref=line_recv,
            send_sem=line_ssem.at[0],
            recv_sem=line_rsem.at[0],
            device_id={"ax": lax.rem(me + 1, n)},
            device_id_type=MESH,
        )

    def one_hot():
        cells = cells_ref[...]
        count = cells.shape[1]
        if width & (width - 1) == 0:
            cell_y = lax.shift_right_logical(cells, width.bit_length() - 1)
            cell_x = cells & (width - 1)
        else:
            cell_y = cells // width
            cell_x = cells - cell_y * width
        rows_y = lax.broadcasted_iota(jnp.int32, (height, count), 0) == cell_y
        rows_x = lax.broadcasted_iota(jnp.int32, (width, count), 0) == cell_x
        at_y[...] = jnp.where(rows_y, 1.0, 0.0).astype(jnp.bfloat16)
        at_x[...] = jnp.where(rows_x, 1.0, 0.0).astype(jnp.bfloat16)

    def inlet():
        all_lines().wait_recv()
        own = line_send[...]
        received = [own] + [line_recv[k] for k in range(n - 1)]
        lines = [
            functools.reduce(jnp.add, received[g * rep : (g + 1) * rep]) for g in range(groups)
        ]
        count = at_y.shape[1]
        lit = at_y[...]
        terms = []
        rest = jnp.concatenate(
            [
                jnp.concatenate([v[j] for v in lines], axis=1)
                for j in range(3)
            ]
            + [jnp.zeros((8 - 3 * steps, count), jnp.float32)] * (3 * steps < 8),
            axis=0,
        )
        for _ in range(3):
            head = rest.astype(jnp.bfloat16)
            rest = rest - head.astype(jnp.float32)
            head = head.astype(jnp.float32)
            terms += [
                lit * jnp.broadcast_to(head[r : r + 1], lit.shape).astype(jnp.bfloat16)
                for r in range(3 * steps)
            ]
        found = lax.dot_general(
            jnp.concatenate(terms, axis=0),
            at_x[...],
            (((1,), (1,)), ((), ())),
            preferred_element_type=jnp.float32,
        )
        size = 3 * steps * height
        plane = found[:size] + (found[size : 2 * size] + found[2 * size :])
        for s in range(steps):
            v = [
                inflow_scale * plane[(steps * j + s) * height : (steps * j + s + 1) * height]
                for j in range(3)
            ]
            speed_sq = v[0] * v[0] + v[1] * v[1] + v[2] * v[2]
            for k, i in enumerate(up_dirs):
                along = v[2]
                for axis in range(2):
                    if lattice_c[i][axis] > 0:
                        along = along + v[axis]
                    elif lattice_c[i][axis] < 0:
                        along = along - v[axis]
                low[s, k, rows, :] = lattice_w[i] * (
                    1.0 + 3.0 * along + 4.5 * along * along - 1.5 * speed_sq
                )

    loads[planes - 1].wait()
    solid_load.wait()
    for z in range(planes - 1, -1, -1):
        if z < planes - 1:
            loads[z].wait()
        collide(0, z)
    cells_load.wait()
    pl.when(me == 0)(one_hot)
    pl.semaphore_wait(barrier, n - 1)

    def part_start(k, carry):
        part_copy(k).start()
        return carry

    lax.fori_loop(1, n, part_start, 0)
    send_up(0)
    send_down(0)
    flags_load.wait()

    def early(s, z, flat):
        dirs = [
            i
            for i in range(19)
            if (lattice_c[i][2] == 0) == flat and 0 <= z - lattice_c[i][2] < planes
        ]
        stream(s, z, dirs)

    for z in range(planes):
        early(0, z, True)
    for s in range(steps):
        last = s == steps - 1
        for z in range(planes - 1, -1, -1):
            early(s, z, False)
        if s == 0:
            all_parts().wait_recv()
            total = part_send[...] + jnp.sum(part_recv[...], axis=0)
            total = jnp.concatenate([total, jnp.zeros((8 - steps, modes), jnp.float32)], axis=0)
            basis = jnp.concatenate([pod_ref[j] for j in range(3)], axis=0)
            if 3 * local < LANES:
                basis = jnp.concatenate(
                    [basis, jnp.zeros((LANES - 3 * local, modes), jnp.float32)], axis=0
                )
            lines = split_dot(total, basis, (((1,), (1,)), ((), ())))
            lane = lax.broadcasted_iota(jnp.int32, (steps, LANES), 1)
            first = lax.rem(me, rep) * local
            mine = (lane >= first) & (lane < first + local)
            for j in range(3):
                inflow_ref[j] = lines[:steps, j * local : (j + 1) * local]
                turn = lax.rem(first + (LANES - j * local), LANES)
                line_send[j] = jnp.where(mine, pltpu.roll(lines, turn, 1)[:steps], 0.0)

            @pl.when(me > 0)
            def _():
                line_copy(me).start()

        for z in range(planes - 1, -1, -1):
            if z == planes - 1:

                @pl.when(me < n - 1)
                def _():
                    down_copy(s).wait_recv()

                @pl.when(me == n - 1)
                def _():
                    for k in range(CROSS):
                        high[s, k, rows, :] = r_buf[s, CROSS + k, planes - 1, rows, :]

                stream(s, z, down_dirs)
            if z == 0:
                if s == 0:
                    pl.when(me == 0)(inlet)

                @pl.when(me > 0)
                def _():
                    up_copy(s).wait_recv()

                stream(s, z, up_dirs)
            if not last:
                collide(s + 1, z)
                if z == planes - 1:
                    send_up(s + 1)
                if z == 0:
                    send_down(s + 1)
                early(s + 1, z, True)

    all_parts().wait_send()

    @pl.when(me > 0)
    def _():
        line_copy(me).wait_send()
        for s in range(steps):
            down_copy(s).wait_send()

    @pl.when(me < n - 1)
    def _():
        for s in range(steps):
            up_copy(s).wait_send()


def finish(f_ref, inflow_ref, out_hbm, inflow_hbm, sem):
    count = f_ref.shape[0]
    small = pltpu.make_async_copy(inflow_ref, inflow_hbm, sem.at[1])
    small.start()
    for i in range(count):
        pltpu.make_async_copy(f_ref.at[i], out_hbm.at[i], sem.at[0]).start()
    pltpu.make_async_copy(f_ref, out_hbm, sem.at[0]).wait()
    small.wait()


def body(n, populations, solid_mask, link_flags, inlet_cells, pod_basis, mri_frames, frame_index):
    planes, height, width = solid_mask.shape
    modes, _, local = pod_basis.shape
    if planes < 2 or LANES % local or n % (LANES // local) or width != LANES or height % 16:
        raise ValueError("sizes")
    dma = pltpu.SemaphoreType.DMA
    f32 = jnp.float32
    wide = pltpu.CompilerParams(vmem_limit_bytes=32 * 1024 * 1024)
    on_chip = pl.BlockSpec(memory_space=pltpu.VMEM)
    in_hbm = pl.BlockSpec(memory_space=pltpu.HBM)
    anywhere = pl.BlockSpec(memory_space=pl.ANY)
    advanced, inflow = pl.pallas_call(
        functools.partial(kernel, n),
        name="lattice",
        out_shape=(
            pltpu.VMEM(populations.shape, f32),
            pltpu.VMEM((3, STEPS, local), f32),
        ),
        in_specs=[pl.BlockSpec(memory_space=pltpu.SMEM)] + [in_hbm] * 6,
        out_specs=(on_chip, on_chip),
        scratch_shapes=[
            pltpu.VMEM((1, inlet_cells.shape[0]), jnp.int32),
            pltpu.VMEM((3, local, modes), f32),
            pltpu.VMEM((3, mri_frames.shape[0], local), f32),
            pltpu.VMEM((height, inlet_cells.shape[0]), jnp.bfloat16),
            pltpu.VMEM((width, inlet_cells.shape[0]), jnp.bfloat16),
            pltpu.VMEM((planes, height, width), jnp.int32),
            pltpu.VMEM((2, planes, height, width), jnp.int32),
            pltpu.VMEM((STEPS, 19, planes, height + 2 * PAD, width), f32),
            pltpu.VMEM((STEPS, CROSS, height + 2 * PAD, width), f32),
            pltpu.VMEM((STEPS, CROSS, height + 2 * PAD, width), f32),
            pltpu.VMEM((STEPS, modes), f32),
            pltpu.VMEM((n - 1, STEPS, modes), f32),
            pltpu.VMEM((3, STEPS, LANES), f32),
            pltpu.VMEM((n - 1, 3, STEPS, LANES), f32),
            dma((planes,)),
            dma((5,)),
            dma((1,)),
            dma((1,)),
            dma((1,)),
            dma((1,)),
            dma((STEPS,)),
            dma((STEPS,)),
            dma((STEPS,)),
            dma((STEPS,)),
        ],
        compiler_params=pltpu.CompilerParams(
            collective_id=0, has_side_effects=True, vmem_limit_bytes=32 * 1024 * 1024
        ),
    )(
        frame_index,
        *(
            pltpu.with_memory_space_constraint(operand, pltpu.HBM)
            for operand in (
                populations,
                solid_mask,
                link_flags,
                inlet_cells.reshape(1, -1),
                jnp.transpose(pod_basis, (1, 2, 0)),
                jnp.transpose(mri_frames, (1, 0, 2)),
            )
        )
    )
    advanced, inflow = pl.pallas_call(
        finish,
        name="finish",
        out_shape=(
            jax.ShapeDtypeStruct(populations.shape, f32),
            jax.ShapeDtypeStruct((3, STEPS, local), f32),
        ),
        in_specs=[on_chip, on_chip],
        out_specs=(anywhere, anywhere),
        scratch_shapes=[dma((2,))],
        compiler_params=wide,
    )(advanced, inflow)
    return advanced, jnp.transpose(inflow, (1, 0, 2))


def solution(mesh):
    in_specs = (
        P(None, "ax", "case", None),
        P("ax", "case", None),
        P(None, "ax", "case", None),
        P("case"),
        P(None, None, "ax"),
        P(None, "case", "ax"),
        P(),
    )
    out_specs = (P(None, "ax", "case", None), P(None, "case", "ax"))
    return jax.shard_map(
        functools.partial(body, mesh.shape["ax"]),
        mesh=mesh,
        in_specs=in_specs,
        out_specs=out_specs,
        check_vma=False,
    )
```

```python
import functools
import math

import jax
import jax.numpy as jnp
from jax import lax
from jax.experimental import pallas as pl
from jax.experimental.pallas import tpu as pltpu
from jax.sharding import PartitionSpec as P

STEPS = 2
MESH = pl.DeviceIdType.MESH
PAD = 8
LANES = 128

lattice_c = (
    (0, 0, 0),
    (1, 0, 0),
    (-1, 0, 0),
    (0, 1, 0),
    (0, -1, 0),
    (0, 0, 1),
    (0, 0, -1),
    (1, 1, 0),
    (-1, -1, 0),
    (1, -1, 0),
    (-1, 1, 0),
    (1, 0, 1),
    (-1, 0, -1),
    (1, 0, -1),
    (-1, 0, 1),
    (0, 1, 1),
    (0, -1, -1),
    (0, 1, -1),
    (0, -1, 1),
)
lattice_w = (1.0 / 3.0,) + (1.0 / 18.0,) * 6 + (1.0 / 36.0,) * 12
opposite_of = (0, 2, 1, 4, 3, 6, 5, 8, 7, 10, 9, 12, 11, 14, 13, 16, 15, 18, 17)
relax_base = 0.52
smagorinsky_sq = 0.04
inflow_scale = 0.05

up_dirs = tuple(i for i in range(19) if lattice_c[i][2] == 1)
down_dirs = tuple(i for i in range(19) if lattice_c[i][2] == -1)
flat_dirs = tuple(i for i in range(19) if lattice_c[i][2] == 0)
slot_of = {d: k for k, d in enumerate(up_dirs + down_dirs + flat_dirs)}
CROSS = len(up_dirs)


def split_dot(left, right, dims):
    dot = functools.partial(
        lax.dot_general, dimension_numbers=dims, preferred_element_type=jnp.float32
    )
    rows = left.shape[0]
    left_high = left.astype(jnp.bfloat16)
    left_low = (left - left_high.astype(jnp.float32)).astype(jnp.bfloat16)
    right_high = right.astype(jnp.bfloat16)
    right_low = (right - right_high.astype(jnp.float32)).astype(jnp.bfloat16)
    both = dot(jnp.concatenate([left_high, left_low], axis=0), right_high)
    return both[:rows] + (both[rows:] + dot(left_high, right_low))


def relax(f, solid):
    pair = [f[i] + f[i + 1] for i in range(1, 19, 2)]
    diff = [f[i] - f[i + 1] for i in range(1, 19, 2)]
    in_xy = pair[3] + pair[4]
    in_xz = pair[5] + pair[6]
    in_yz = pair[7] + pair[8]
    density = (f[0] + pair[0]) + (pair[1] + pair[2]) + (in_xy + in_xz) + in_yz
    flux = (
        diff[0] + (diff[3] + diff[4]) + (diff[5] + diff[6]),
        diff[1] + (diff[3] - diff[4]) + (diff[7] + diff[8]),
        diff[2] + (diff[5] - diff[6]) + (diff[7] - diff[8]),
    )
    inverse = 1.0 / density
    speed = [j * inverse for j in flux]
    third = density * (1.0 / 3.0)
    square = [j * u for j, u in zip(flux, speed)]
    s_xx = pair[0] + in_xy + in_xz - third - square[0]
    s_yy = pair[1] + in_xy + in_yz - third - square[1]
    s_zz = pair[2] + in_xz + in_yz - third - square[2]
    s_xy = pair[3] - pair[4] - flux[0] * speed[1]
    s_xz = pair[5] - pair[6] - flux[0] * speed[2]
    s_yz = pair[7] - pair[8] - flux[1] * speed[2]
    magnitude = (s_xx * s_xx + s_yy * s_yy + s_zz * s_zz) + 2.0 * (
        s_xy * s_xy + s_xz * s_xz + s_yz * s_yz
    )
    root = jnp.sqrt(
        relax_base * relax_base
        + (18.0 * math.sqrt(2.0) * smagorinsky_sq) * jnp.sqrt(magnitude) * inverse
    )
    rate = jnp.where(solid == 1, 0.0, 2.0 / (relax_base + root))
    keep = 1.0 - rate
    base = density - 1.5 * (square[0] + square[1] + square[2])
    by_axis = rate * (1.0 / 18.0)
    by_edge = rate * (1.0 / 36.0)
    triple = [3.0 * j for j in flux]
    out = [keep * f[0] + (rate * (1.0 / 3.0)) * base]
    for i in range(1, 19, 2):
        c = lattice_c[i]
        along = moved = None
        for axis in range(3):
            if c[axis] == 0:
                continue
            if along is None:
                along, moved = speed[axis], triple[axis]
            elif c[axis] > 0:
                along, moved = along + speed[axis], moved + triple[axis]
            else:
                along, moved = along - speed[axis], moved - triple[axis]
        even = base + 1.5 * (moved * along)
        weight = by_axis if i < 7 else by_edge
        out.append(keep * f[i] + weight * (even + moved))
        out.append(keep * f[i + 1] + weight * (even - moved))
    return out


def kernel(
    n,
    frame_ref,
    f_hbm,
    solid_hbm,
    flags_hbm,
    cells_hbm,
    pod_hbm,
    mri_hbm,
    f_buf,
    inflow_ref,
    cells_ref,
    pod_ref,
    mri_ref,
    at_y,
    at_x,
    solid_buf,
    flags_buf,
    r_buf,
    low,
    high,
    part_send,
    part_recv,
    line_send,
    line_recv,
    in_sem,
    mask_sem,
    part_ssem,
    part_rsem,
    line_ssem,
    line_rsem,
    up_ssem,
    up_rsem,
    down_ssem,
    down_rsem,
):
    planes, height, width = solid_buf.shape
    steps = STEPS
    frames = mri_ref.shape[1]
    local = mri_ref.shape[2]
    modes = pod_ref.shape[2]
    rep = LANES // local
    groups = n // rep
    chunk = 16
    rows = slice(PAD, PAD + height)
    me = lax.axis_index("ax")

    barrier = pltpu.get_barrier_semaphore()

    def greet(k, carry):
        pl.semaphore_signal(
            barrier, inc=1, device_id={"ax": lax.rem(me + k, n)}, device_id_type=MESH
        )
        return carry

    lax.fori_loop(1, n, greet, 0)

    loads = []
    for z in range(planes):
        loads.append(pltpu.make_async_copy(f_hbm.at[:, z], f_buf.at[:, z], in_sem.at[z]))
    solid_load = pltpu.make_async_copy(solid_hbm, solid_buf, mask_sem.at[0])
    flags_load = pltpu.make_async_copy(flags_hbm, flags_buf, mask_sem.at[1])
    pod_load = pltpu.make_async_copy(pod_hbm, pod_ref, mask_sem.at[2])
    mri_load = pltpu.make_async_copy(mri_hbm, mri_ref, mask_sem.at[3])
    cells_load = pltpu.make_async_copy(cells_hbm, cells_ref, mask_sem.at[4])
    mri_load.start()
    pod_load.start()
    loads[planes - 1].start()
    solid_load.start()
    for z in range(planes - 2, -1, -1):
        loads[z].start()
    flags_load.start()
    cells_load.start()
    mri_load.wait()
    pod_load.wait()

    row_at = lax.broadcasted_iota(jnp.int32, (8, local), 0)
    frame_at = lax.broadcasted_iota(jnp.int32, (frames, local), 0)
    partial = jnp.zeros((8, modes), jnp.float32)
    for j in range(3):
        chosen = jnp.zeros((8, local), jnp.float32)
        for s in range(steps):
            frame = lax.rem(frame_ref[0] + s, frames)
            line = jnp.sum(jnp.where(frame_at == frame, mri_ref[j], 0.0), axis=0, keepdims=True)
            chosen = jnp.where(row_at == s, line, chosen)
        partial = partial + split_dot(chosen, pod_ref[j], (((1,), (0,)), ((), ())))
    part_send[...] = partial[:steps]

    def collide(s, z, first=0, count=None):
        def at(c, carry):
            r0 = pl.multiple_of(c * chunk, chunk)
            here = pl.ds(r0, chunk)
            there = pl.ds(pl.multiple_of(r0 + PAD, 8), chunk)
            f = [f_buf[i, z, here, :] for i in range(19)]
            relaxed = relax(f, solid_buf[z, here, :])
            for i in range(19):
                r_buf[s, slot_of[i], z, there, :] = relaxed[i]
            return carry

        lax.fori_loop(first, height // chunk if count is None else first + count, at, 0)

    def up_copy(s, start=0, size=None):
        span = pl.ds(PAD + start, height if size is None else size)
        return pltpu.make_async_remote_copy(
            src_ref=r_buf.at[s, pl.ds(0, CROSS), planes - 1, span],
            dst_ref=low.at[s, :, span],
            send_sem=up_ssem.at[s],
            recv_sem=up_rsem.at[s],
            device_id={"ax": lax.rem(me + 1, n)},
            device_id_type=MESH,
        )

    def down_copy(s, start=0, size=None):
        span = pl.ds(PAD + start, height if size is None else size)
        return pltpu.make_async_remote_copy(
            src_ref=r_buf.at[s, pl.ds(CROSS, CROSS), 0, span],
            dst_ref=high.at[s, :, span],
            send_sem=down_ssem.at[s],
            recv_sem=down_rsem.at[s],
            device_id={"ax": lax.rem(me + n - 1, n)},
            device_id_type=MESH,
        )

    def part_copy(k):
        return pltpu.make_async_remote_copy(
            src_ref=part_send,
            dst_ref=part_recv.at[k - 1],
            send_sem=part_ssem.at[0],
            recv_sem=part_rsem.at[0],
            device_id={"ax": lax.rem(me + k, n)},
            device_id_type=MESH,
        )

    def all_parts():
        return pltpu.make_async_remote_copy(
            src_ref=part_recv,
            dst_ref=part_recv,
            send_sem=part_ssem.at[0],
            recv_sem=part_rsem.at[0],
            device_id={"ax": lax.rem(me + 1, n)},
            device_id_type=MESH,
        )

    def line_copy(source):
        return pltpu.make_async_remote_copy(
            src_ref=line_send,
            dst_ref=line_recv.at[source - 1],
            send_sem=line_ssem.at[0],
            recv_sem=line_rsem.at[0],
            device_id={"ax": 0},
            device_id_type=MESH,
        )

    def send_up(s, start=0, size=None):
        @pl.when(me < n - 1)
        def _():
            up_copy(s, start, size).start()

    def send_down(s, start=0, size=None):
        @pl.when(me > 0)
        def _():
            down_copy(s, start, size).start()

    def stream(s, z, dirs):
        solid = solid_buf[z] == 1
        for i in dirs:
            step_x, step_y, step_z = lattice_c[i]
            own = r_buf[s, slot_of[i], z, rows, :]
            if i == 0:
                f_buf[i, z] = own
                continue
            moved = slice(PAD - step_y, PAD - step_y + height)
            if 0 <= z - step_z < planes:
                source = r_buf[s, slot_of[i], z - step_z, moved, :]
            elif step_z > 0:
                source = low[s, slot_of[i], moved, :]
            else:
                source = high[s, slot_of[i] - CROSS, moved, :]
            if step_x != 0:
                source = pltpu.roll(source, step_x % width, 1)
            bit = 1 << ((i - 1) % 9)
            linked = (flags_buf[(i - 1) // 9, z] & bit) != 0
            back = r_buf[s, slot_of[opposite_of[i]], z, rows, :]
            f_buf[i, z] = jnp.where(solid, own, jnp.where(linked, back, source))

    def all_lines():
        return pltpu.make_async_remote_copy(
            src_ref=line_recv,
            dst_ref=line_recv,
            send_sem=line_ssem.at[0],
            recv_sem=line_rsem.at[0],
            device_id={"ax": lax.rem(me + 1, n)},
            device_id_type=MESH,
        )

    def one_hot():
        cells = cells_ref[...]
        count = cells.shape[1]
        if width & (width - 1) == 0:
            cell_y = lax.shift_right_logical(cells, width.bit_length() - 1)
            cell_x = cells & (width - 1)
        else:
            cell_y = cells // width
            cell_x = cells - cell_y * width
        rows_y = lax.broadcasted_iota(jnp.int32, (height, count), 0) == cell_y
        rows_x = lax.broadcasted_iota(jnp.int32, (width, count), 0) == cell_x
        at_y[...] = jnp.where(rows_y, 1.0, 0.0).astype(jnp.bfloat16)
        at_x[...] = jnp.where(rows_x, 1.0, 0.0).astype(jnp.bfloat16)

    def inlet():
        all_lines().wait_recv()
        own = line_send[...]
        received = [own] + [line_recv[k] for k in range(n - 1)]
        lines = [
            functools.reduce(jnp.add, received[g * rep : (g + 1) * rep]) for g in range(groups)
        ]
        count = at_y.shape[1]
        lit = at_y[...]
        terms = []
        rest = jnp.concatenate(
            [
                jnp.concatenate([v[j] for v in lines], axis=1)
                for j in range(3)
            ]
            + [jnp.zeros((8 - 3 * steps, count), jnp.float32)] * (3 * steps < 8),
            axis=0,
        )
        for _ in range(3):
            head = rest.astype(jnp.bfloat16)
            rest = rest - head.astype(jnp.float32)
            head = head.astype(jnp.float32)
            terms += [
                lit * jnp.broadcast_to(head[r : r + 1], lit.shape).astype(jnp.bfloat16)
                for r in range(3 * steps)
            ]
        found = lax.dot_general(
            jnp.concatenate(terms, axis=0),
            at_x[...],
            (((1,), (1,)), ((), ())),
            preferred_element_type=jnp.float32,
        )
        size = 3 * steps * height
        plane = found[:size] + (found[size : 2 * size] + found[2 * size :])
        for s in range(steps):
            v = [
                inflow_scale * plane[(steps * j + s) * height : (steps * j + s + 1) * height]
                for j in range(3)
            ]
            speed_sq = v[0] * v[0] + v[1] * v[1] + v[2] * v[2]
            for k, i in enumerate(up_dirs):
                along = v[2]
                for axis in range(2):
                    if lattice_c[i][axis] > 0:
                        along = along + v[axis]
                    elif lattice_c[i][axis] < 0:
                        along = along - v[axis]
                low[s, k, rows, :] = lattice_w[i] * (
                    1.0 + 3.0 * along + 4.5 * along * along - 1.5 * speed_sq
                )

    loads[planes - 1].wait()
    solid_load.wait()
    for z in range(planes - 1, -1, -1):
        if z < planes - 1:
            loads[z].wait()
        collide(0, z)
    cells_load.wait()
    pl.when(me == 0)(one_hot)
    pl.semaphore_wait(barrier, n - 1)

    def part_start(k, carry):
        part_copy(k).start()
        return carry

    lax.fori_loop(1, n, part_start, 0)
    send_up(0)
    send_down(0)
    flags_load.wait()

    def early(s, z, flat):
        dirs = [
            i
            for i in range(19)
            if (lattice_c[i][2] == 0) == flat and 0 <= z - lattice_c[i][2] < planes
        ]
        stream(s, z, dirs)

    for z in range(planes):
        early(0, z, True)
    for s in range(steps):
        last = s == steps - 1
        for z in range(planes - 1, -1, -1):
            early(s, z, False)
        if s == 0:
            all_parts().wait_recv()
            total = part_send[...] + jnp.sum(part_recv[...], axis=0)
            total = jnp.concatenate([total, jnp.zeros((8 - steps, modes), jnp.float32)], axis=0)
            basis = jnp.concatenate([pod_ref[j] for j in range(3)], axis=0)
            if 3 * local < LANES:
                basis = jnp.concatenate(
                    [basis, jnp.zeros((LANES - 3 * local, modes), jnp.float32)], axis=0
                )
            lines = split_dot(total, basis, (((1,), (1,)), ((), ())))
            lane = lax.broadcasted_iota(jnp.int32, (steps, LANES), 1)
            first = lax.rem(me, rep) * local
            mine = (lane >= first) & (lane < first + local)
            for j in range(3):
                inflow_ref[j] = lines[:steps, j * local : (j + 1) * local]
                turn = lax.rem(first + (LANES - j * local), LANES)
                line_send[j] = jnp.where(mine, pltpu.roll(lines, turn, 1)[:steps], 0.0)

            @pl.when(me > 0)
            def _():
                line_copy(me).start()

        for z in range(planes - 1, -1, -1):
            if z == planes - 1:

                @pl.when(me < n - 1)
                def _():
                    down_copy(s).wait_recv()

                @pl.when(me == n - 1)
                def _():
                    for k in range(CROSS):
                        high[s, k, rows, :] = r_buf[s, CROSS + k, planes - 1, rows, :]

                stream(s, z, down_dirs)
            if z == 0:
                if s == 0:
                    pl.when(me == 0)(inlet)

                @pl.when(me > 0)
                def _():
                    up_copy(s).wait_recv()

                stream(s, z, up_dirs)
            if not last:
                for c in range(height // chunk):
                    collide(s + 1, z, c, 1)
                    if z == planes - 1:
                        send_up(s + 1, c * chunk, chunk)
                    if z == 0:
                        send_down(s + 1, c * chunk, chunk)
                early(s + 1, z, True)

    all_parts().wait_send()

    @pl.when(me > 0)
    def _():
        line_copy(me).wait_send()
        for s in range(steps):
            down_copy(s).wait_send()

    @pl.when(me < n - 1)
    def _():
        for s in range(steps):
            up_copy(s).wait_send()


def finish(f_ref, inflow_ref, out_hbm, inflow_hbm, sem):
    count = f_ref.shape[0]
    small = pltpu.make_async_copy(inflow_ref, inflow_hbm, sem.at[1])
    small.start()
    for i in range(count):
        pltpu.make_async_copy(f_ref.at[i], out_hbm.at[i], sem.at[0]).start()
    pltpu.make_async_copy(f_ref, out_hbm, sem.at[0]).wait()
    small.wait()


def body(n, populations, solid_mask, link_flags, inlet_cells, pod_basis, mri_frames, frame_index):
    planes, height, width = solid_mask.shape
    modes, _, local = pod_basis.shape
    if planes < 2 or LANES % local or n % (LANES // local) or width != LANES or height % 16:
        raise ValueError("sizes")
    dma = pltpu.SemaphoreType.DMA
    f32 = jnp.float32
    wide = pltpu.CompilerParams(vmem_limit_bytes=32 * 1024 * 1024)
    on_chip = pl.BlockSpec(memory_space=pltpu.VMEM)
    in_hbm = pl.BlockSpec(memory_space=pltpu.HBM)
    anywhere = pl.BlockSpec(memory_space=pl.ANY)
    advanced, inflow = pl.pallas_call(
        functools.partial(kernel, n),
        name="lattice",
        out_shape=(
            pltpu.VMEM(populations.shape, f32),
            pltpu.VMEM((3, STEPS, local), f32),
        ),
        in_specs=[pl.BlockSpec(memory_space=pltpu.SMEM)] + [in_hbm] * 6,
        out_specs=(on_chip, on_chip),
        scratch_shapes=[
            pltpu.VMEM((1, inlet_cells.shape[0]), jnp.int32),
            pltpu.VMEM((3, local, modes), f32),
            pltpu.VMEM((3, mri_frames.shape[0], local), f32),
            pltpu.VMEM((height, inlet_cells.shape[0]), jnp.bfloat16),
            pltpu.VMEM((width, inlet_cells.shape[0]), jnp.bfloat16),
            pltpu.VMEM((planes, height, width), jnp.int32),
            pltpu.VMEM((2, planes, height, width), jnp.int32),
            pltpu.VMEM((STEPS, 19, planes, height + 2 * PAD, width), f32),
            pltpu.VMEM((STEPS, CROSS, height + 2 * PAD, width), f32),
            pltpu.VMEM((STEPS, CROSS, height + 2 * PAD, width), f32),
            pltpu.VMEM((STEPS, modes), f32),
            pltpu.VMEM((n - 1, STEPS, modes), f32),
            pltpu.VMEM((3, STEPS, LANES), f32),
            pltpu.VMEM((n - 1, 3, STEPS, LANES), f32),
            dma((planes,)),
            dma((5,)),
            dma((1,)),
            dma((1,)),
            dma((1,)),
            dma((1,)),
            dma((STEPS,)),
            dma((STEPS,)),
            dma((STEPS,)),
            dma((STEPS,)),
        ],
        compiler_params=pltpu.CompilerParams(
            collective_id=0, has_side_effects=True, vmem_limit_bytes=32 * 1024 * 1024
        ),
    )(
        frame_index,
        *(
            pltpu.with_memory_space_constraint(operand, pltpu.HBM)
            for operand in (
                populations,
                solid_mask,
                link_flags,
                inlet_cells.reshape(1, -1),
                jnp.transpose(pod_basis, (1, 2, 0)),
                jnp.transpose(mri_frames, (1, 0, 2)),
            )
        )
    )
    advanced, inflow = pl.pallas_call(
        finish,
        name="finish",
        out_shape=(
            jax.ShapeDtypeStruct(populations.shape, f32),
            jax.ShapeDtypeStruct((3, STEPS, local), f32),
        ),
        in_specs=[on_chip, on_chip],
        out_specs=(anywhere, anywhere),
        scratch_shapes=[dma((2,))],
        compiler_params=wide,
    )(advanced, inflow)
    return advanced, jnp.transpose(inflow, (1, 0, 2))


def solution(mesh):
    in_specs = (
        P(None, "ax", "case", None),
        P("ax", "case", None),
        P(None, "ax", "case", None),
        P("case"),
        P(None, None, "ax"),
        P(None, "case", "ax"),
        P(),
    )
    out_specs = (P(None, "ax", "case", None), P(None, "case", "ax"))
    return jax.shard_map(
        functools.partial(body, mesh.shape["ax"]),
        mesh=mesh,
        in_specs=in_specs,
        out_specs=out_specs,
        check_vma=False,
    )
```

```python
import functools
import math

import jax
import jax.numpy as jnp
from jax import lax
from jax.experimental import pallas as pl
from jax.experimental.pallas import tpu as pltpu
from jax.sharding import PartitionSpec as P

STEPS = 2
MESH = pl.DeviceIdType.MESH
PAD = 8
LANES = 128

lattice_c = (
    (0, 0, 0),
    (1, 0, 0),
    (-1, 0, 0),
    (0, 1, 0),
    (0, -1, 0),
    (0, 0, 1),
    (0, 0, -1),
    (1, 1, 0),
    (-1, -1, 0),
    (1, -1, 0),
    (-1, 1, 0),
    (1, 0, 1),
    (-1, 0, -1),
    (1, 0, -1),
    (-1, 0, 1),
    (0, 1, 1),
    (0, -1, -1),
    (0, 1, -1),
    (0, -1, 1),
)
lattice_w = (1.0 / 3.0,) + (1.0 / 18.0,) * 6 + (1.0 / 36.0,) * 12
opposite_of = (0, 2, 1, 4, 3, 6, 5, 8, 7, 10, 9, 12, 11, 14, 13, 16, 15, 18, 17)
relax_base = 0.52
smagorinsky_sq = 0.04
inflow_scale = 0.05

up_dirs = tuple(i for i in range(19) if lattice_c[i][2] == 1)
down_dirs = tuple(i for i in range(19) if lattice_c[i][2] == -1)
flat_dirs = tuple(i for i in range(19) if lattice_c[i][2] == 0)
slot_of = {d: k for k, d in enumerate(up_dirs + down_dirs + flat_dirs)}
CROSS = len(up_dirs)


def split_dot(left, right, dims):
    dot = functools.partial(
        lax.dot_general, dimension_numbers=dims, preferred_element_type=jnp.float32
    )
    rows = left.shape[0]
    left_high = left.astype(jnp.bfloat16)
    left_low = (left - left_high.astype(jnp.float32)).astype(jnp.bfloat16)
    right_high = right.astype(jnp.bfloat16)
    right_low = (right - right_high.astype(jnp.float32)).astype(jnp.bfloat16)
    both = dot(jnp.concatenate([left_high, left_low], axis=0), right_high)
    return both[:rows] + (both[rows:] + dot(left_high, right_low))


def relax(f, solid):
    pair = [f[i] + f[i + 1] for i in range(1, 19, 2)]
    diff = [f[i] - f[i + 1] for i in range(1, 19, 2)]
    in_xy = pair[3] + pair[4]
    in_xz = pair[5] + pair[6]
    in_yz = pair[7] + pair[8]
    density = (f[0] + pair[0]) + (pair[1] + pair[2]) + (in_xy + in_xz) + in_yz
    flux = (
        diff[0] + (diff[3] + diff[4]) + (diff[5] + diff[6]),
        diff[1] + (diff[3] - diff[4]) + (diff[7] + diff[8]),
        diff[2] + (diff[5] - diff[6]) + (diff[7] - diff[8]),
    )
    inverse = 1.0 / density
    speed = [j * inverse for j in flux]
    third = density * (1.0 / 3.0)
    square = [j * u for j, u in zip(flux, speed)]
    s_xx = pair[0] + in_xy + in_xz - third - square[0]
    s_yy = pair[1] + in_xy + in_yz - third - square[1]
    s_zz = pair[2] + in_xz + in_yz - third - square[2]
    s_xy = pair[3] - pair[4] - flux[0] * speed[1]
    s_xz = pair[5] - pair[6] - flux[0] * speed[2]
    s_yz = pair[7] - pair[8] - flux[1] * speed[2]
    magnitude = (s_xx * s_xx + s_yy * s_yy + s_zz * s_zz) + 2.0 * (
        s_xy * s_xy + s_xz * s_xz + s_yz * s_yz
    )
    root = jnp.sqrt(
        relax_base * relax_base
        + (18.0 * math.sqrt(2.0) * smagorinsky_sq) * jnp.sqrt(magnitude) * inverse
    )
    rate = jnp.where(solid == 1, 0.0, 2.0 / (relax_base + root))
    keep = 1.0 - rate
    base = density - 1.5 * (square[0] + square[1] + square[2])
    by_axis = rate * (1.0 / 18.0)
    by_edge = rate * (1.0 / 36.0)
    triple = [3.0 * j for j in flux]
    out = [keep * f[0] + (rate * (1.0 / 3.0)) * base]
    for i in range(1, 19, 2):
        c = lattice_c[i]
        along = moved = None
        for axis in range(3):
            if c[axis] == 0:
                continue
            if along is None:
                along, moved = speed[axis], triple[axis]
            elif c[axis] > 0:
                along, moved = along + speed[axis], moved + triple[axis]
            else:
                along, moved = along - speed[axis], moved - triple[axis]
        even = base + 1.5 * (moved * along)
        weight = by_axis if i < 7 else by_edge
        out.append(keep * f[i] + weight * (even + moved))
        out.append(keep * f[i + 1] + weight * (even - moved))
    return out


def kernel(
    n,
    frame_ref,
    f_hbm,
    solid_hbm,
    flags_hbm,
    cells_hbm,
    pod_hbm,
    mri_hbm,
    f_buf,
    inflow_ref,
    cells_ref,
    pod_ref,
    mri_ref,
    at_y,
    at_x,
    solid_buf,
    flags_buf,
    r_buf,
    low,
    high,
    part_send,
    part_recv,
    line_send,
    line_recv,
    in_sem,
    mask_sem,
    part_ssem,
    part_rsem,
    line_ssem,
    line_rsem,
    up_ssem,
    up_rsem,
    down_ssem,
    down_rsem,
):
    planes, height, width = solid_buf.shape
    steps = STEPS
    frames = mri_ref.shape[1]
    local = mri_ref.shape[2]
    modes = pod_ref.shape[2]
    rep = LANES // local
    groups = n // rep
    chunk = 16
    rows = slice(PAD, PAD + height)
    me = lax.axis_index("ax")

    barrier = pltpu.get_barrier_semaphore()

    def greet(k, carry):
        pl.semaphore_signal(
            barrier, inc=1, device_id={"ax": lax.rem(me + k, n)}, device_id_type=MESH
        )
        return carry

    lax.fori_loop(1, n, greet, 0)

    loads = []
    for z in range(planes):
        loads.append(pltpu.make_async_copy(f_hbm.at[:, z], f_buf.at[:, z], in_sem.at[z]))
    solid_load = pltpu.make_async_copy(solid_hbm, solid_buf, mask_sem.at[0])
    flags_load = pltpu.make_async_copy(flags_hbm, flags_buf, mask_sem.at[1])
    pod_load = pltpu.make_async_copy(pod_hbm, pod_ref, mask_sem.at[2])
    mri_load = pltpu.make_async_copy(mri_hbm, mri_ref, mask_sem.at[3])
    cells_load = pltpu.make_async_copy(cells_hbm, cells_ref, mask_sem.at[4])
    mri_load.start()
    pod_load.start()
    loads[planes - 1].start()
    solid_load.start()
    for z in range(planes - 2, -1, -1):
        loads[z].start()
    flags_load.start()
    cells_load.start()
    mri_load.wait()
    pod_load.wait()

    row_at = lax.broadcasted_iota(jnp.int32, (8, local), 0)
    frame_at = lax.broadcasted_iota(jnp.int32, (frames, local), 0)
    partial = jnp.zeros((8, modes), jnp.float32)
    for j in range(3):
        chosen = jnp.zeros((8, local), jnp.float32)
        for s in range(steps):
            frame = lax.rem(frame_ref[0] + s, frames)
            line = jnp.sum(jnp.where(frame_at == frame, mri_ref[j], 0.0), axis=0, keepdims=True)
            chosen = jnp.where(row_at == s, line, chosen)
        partial = partial + split_dot(chosen, pod_ref[j], (((1,), (0,)), ((), ())))
    part_send[...] = partial[:steps]

    def collide(s, z, first=0, count=None):
        def at(c, carry):
            r0 = pl.multiple_of(c * chunk, chunk)
            here = pl.ds(r0, chunk)
            there = pl.ds(pl.multiple_of(r0 + PAD, 8), chunk)
            f = [f_buf[i, z, here, :] for i in range(19)]
            relaxed = relax(f, solid_buf[z, here, :])
            for i in range(19):
                r_buf[s, slot_of[i], z, there, :] = relaxed[i]
            return carry

        lax.fori_loop(first, height // chunk if count is None else first + count, at, 0)

    def up_copy(s, start=0, size=None):
        span = pl.ds(PAD + start, height if size is None else size)
        return pltpu.make_async_remote_copy(
            src_ref=r_buf.at[s, pl.ds(0, CROSS), planes - 1, span],
            dst_ref=low.at[s, :, span],
            send_sem=up_ssem.at[s],
            recv_sem=up_rsem.at[s],
            device_id={"ax": lax.rem(me + 1, n)},
            device_id_type=MESH,
        )

    def down_copy(s, start=0, size=None):
        span = pl.ds(PAD + start, height if size is None else size)
        return pltpu.make_async_remote_copy(
            src_ref=r_buf.at[s, pl.ds(CROSS, CROSS), 0, span],
            dst_ref=high.at[s, :, span],
            send_sem=down_ssem.at[s],
            recv_sem=down_rsem.at[s],
            device_id={"ax": lax.rem(me + n - 1, n)},
            device_id_type=MESH,
        )

    def part_copy(k):
        return pltpu.make_async_remote_copy(
            src_ref=part_send,
            dst_ref=part_recv.at[k - 1],
            send_sem=part_ssem.at[0],
            recv_sem=part_rsem.at[0],
            device_id={"ax": lax.rem(me + k, n)},
            device_id_type=MESH,
        )

    def all_parts():
        return pltpu.make_async_remote_copy(
            src_ref=part_recv,
            dst_ref=part_recv,
            send_sem=part_ssem.at[0],
            recv_sem=part_rsem.at[0],
            device_id={"ax": lax.rem(me + 1, n)},
            device_id_type=MESH,
        )

    def line_copy(source):
        return pltpu.make_async_remote_copy(
            src_ref=line_send,
            dst_ref=line_recv.at[source - 1],
            send_sem=line_ssem.at[0],
            recv_sem=line_rsem.at[0],
            device_id={"ax": 0},
            device_id_type=MESH,
        )

    def send_up(s, start=0, size=None):
        @pl.when(me < n - 1)
        def _():
            up_copy(s, start, size).start()

    def send_down(s, start=0, size=None):
        @pl.when(me > 0)
        def _():
            down_copy(s, start, size).start()

    def stream(s, z, dirs):
        solid = solid_buf[z] == 1
        for i in dirs:
            step_x, step_y, step_z = lattice_c[i]
            own = r_buf[s, slot_of[i], z, rows, :]
            if i == 0:
                f_buf[i, z] = own
                continue
            moved = slice(PAD - step_y, PAD - step_y + height)
            if 0 <= z - step_z < planes:
                source = r_buf[s, slot_of[i], z - step_z, moved, :]
            elif step_z > 0:
                source = low[s, slot_of[i], moved, :]
            else:
                source = high[s, slot_of[i] - CROSS, moved, :]
            if step_x != 0:
                source = pltpu.roll(source, step_x % width, 1)
            bit = 1 << ((i - 1) % 9)
            linked = (flags_buf[(i - 1) // 9, z] & bit) != 0
            back = r_buf[s, slot_of[opposite_of[i]], z, rows, :]
            f_buf[i, z] = jnp.where(solid, own, jnp.where(linked, back, source))

    def all_lines():
        return pltpu.make_async_remote_copy(
            src_ref=line_recv,
            dst_ref=line_recv,
            send_sem=line_ssem.at[0],
            recv_sem=line_rsem.at[0],
            device_id={"ax": lax.rem(me + 1, n)},
            device_id_type=MESH,
        )

    def one_hot():
        cells = cells_ref[...]
        count = cells.shape[1]
        if width & (width - 1) == 0:
            cell_y = lax.shift_right_logical(cells, width.bit_length() - 1)
            cell_x = cells & (width - 1)
        else:
            cell_y = cells // width
            cell_x = cells - cell_y * width
        rows_y = lax.broadcasted_iota(jnp.int32, (height, count), 0) == cell_y
        rows_x = lax.broadcasted_iota(jnp.int32, (width, count), 0) == cell_x
        at_y[...] = jnp.where(rows_y, 1.0, 0.0).astype(jnp.bfloat16)
        at_x[...] = jnp.where(rows_x, 1.0, 0.0).astype(jnp.bfloat16)

    def inlet():
        all_lines().wait_recv()
        own = line_send[...]
        received = [own] + [line_recv[k] for k in range(n - 1)]
        lines = [
            functools.reduce(jnp.add, received[g * rep : (g + 1) * rep]) for g in range(groups)
        ]
        count = at_y.shape[1]
        lit = at_y[...]
        terms = []
        rest = jnp.concatenate(
            [
                jnp.concatenate([v[j] for v in lines], axis=1)
                for j in range(3)
            ]
            + [jnp.zeros((8 - 3 * steps, count), jnp.float32)] * (3 * steps < 8),
            axis=0,
        )
        for _ in range(3):
            head = rest.astype(jnp.bfloat16)
            rest = rest - head.astype(jnp.float32)
            head = head.astype(jnp.float32)
            terms += [
                lit * jnp.broadcast_to(head[r : r + 1], lit.shape).astype(jnp.bfloat16)
                for r in range(3 * steps)
            ]
        found = lax.dot_general(
            jnp.concatenate(terms, axis=0),
            at_x[...],
            (((1,), (1,)), ((), ())),
            preferred_element_type=jnp.float32,
        )
        size = 3 * steps * height
        plane = found[:size] + (found[size : 2 * size] + found[2 * size :])
        for s in range(steps):
            v = [
                inflow_scale * plane[(steps * j + s) * height : (steps * j + s + 1) * height]
                for j in range(3)
            ]
            speed_sq = v[0] * v[0] + v[1] * v[1] + v[2] * v[2]
            for k, i in enumerate(up_dirs):
                along = v[2]
                for axis in range(2):
                    if lattice_c[i][axis] > 0:
                        along = along + v[axis]
                    elif lattice_c[i][axis] < 0:
                        along = along - v[axis]
                low[s, k, rows, :] = lattice_w[i] * (
                    1.0 + 3.0 * along + 4.5 * along * along - 1.5 * speed_sq
                )

    loads[planes - 1].wait()
    solid_load.wait()
    for z in range(planes - 1, -1, -1):
        if z < planes - 1:
            loads[z].wait()
        collide(0, z)
    cells_load.wait()
    pl.when(me == 0)(one_hot)
    pl.semaphore_wait(barrier, n - 1)

    def part_start(k, carry):
        part_copy(k).start()
        return carry

    lax.fori_loop(1, n, part_start, 0)
    send_up(0)
    send_down(0)
    flags_load.wait()

    def early(s, z, flat):
        dirs = [
            i
            for i in range(19)
            if (lattice_c[i][2] == 0) == flat and 0 <= z - lattice_c[i][2] < planes
        ]
        stream(s, z, dirs)

    for z in range(planes):
        early(0, z, True)
    for s in range(steps):
        last = s == steps - 1
        for z in range(planes - 1, -1, -1):
            early(s, z, False)
        if s == 0:
            all_parts().wait_recv()
            total = part_send[...] + jnp.sum(part_recv[...], axis=0)
            total = jnp.concatenate([total, jnp.zeros((8 - steps, modes), jnp.float32)], axis=0)
            basis = jnp.concatenate([pod_ref[j] for j in range(3)], axis=0)
            if 3 * local < LANES:
                basis = jnp.concatenate(
                    [basis, jnp.zeros((LANES - 3 * local, modes), jnp.float32)], axis=0
                )
            lines = split_dot(total, basis, (((1,), (1,)), ((), ())))
            lane = lax.broadcasted_iota(jnp.int32, (steps, LANES), 1)
            first = lax.rem(me, rep) * local
            mine = (lane >= first) & (lane < first + local)
            for j in range(3):
                inflow_ref[j] = lines[:steps, j * local : (j + 1) * local]
                turn = lax.rem(first + (LANES - j * local), LANES)
                line_send[j] = jnp.where(mine, pltpu.roll(lines, turn, 1)[:steps], 0.0)

            @pl.when(me > 0)
            def _():
                line_copy(me).start()

        for z in range(planes - 1, -1, -1):
            if z == planes - 1:

                @pl.when(me < n - 1)
                def _():
                    down_copy(s).wait_recv()

                @pl.when(me == n - 1)
                def _():
                    for k in range(CROSS):
                        high[s, k, rows, :] = r_buf[s, CROSS + k, planes - 1, rows, :]

                stream(s, z, down_dirs)
            if z == 0:
                if s == 0:
                    pl.when(me == 0)(inlet)

                @pl.when(me > 0)
                def _():
                    up_copy(s).wait_recv()

                stream(s, z, up_dirs)
            if not last:
                for c in range(height // chunk):
                    collide(s + 1, z, c, 1)
                    if z == planes - 1:
                        send_up(s + 1, c * chunk, chunk)
                    if z == 0:
                        send_down(s + 1, c * chunk, chunk)
                if z > 0:
                    pl.when(me == 0)(functools.partial(early, s + 1, z, True))
                else:
                    early(s + 1, 0, True)

                    @pl.when(me > 0)
                    def _():
                        for rest in range(1, planes):
                            early(s + 1, rest, True)

    all_parts().wait_send()

    @pl.when(me > 0)
    def _():
        line_copy(me).wait_send()
        for s in range(steps):
            down_copy(s).wait_send()

    @pl.when(me < n - 1)
    def _():
        for s in range(steps):
            up_copy(s).wait_send()


def finish(f_ref, inflow_ref, out_hbm, inflow_hbm, sem):
    count = f_ref.shape[0]
    small = pltpu.make_async_copy(inflow_ref, inflow_hbm, sem.at[1])
    small.start()
    for i in range(count):
        pltpu.make_async_copy(f_ref.at[i], out_hbm.at[i], sem.at[0]).start()
    pltpu.make_async_copy(f_ref, out_hbm, sem.at[0]).wait()
    small.wait()


def body(n, populations, solid_mask, link_flags, inlet_cells, pod_basis, mri_frames, frame_index):
    planes, height, width = solid_mask.shape
    modes, _, local = pod_basis.shape
    if planes < 2 or LANES % local or n % (LANES // local) or width != LANES or height % 16:
        raise ValueError("sizes")
    dma = pltpu.SemaphoreType.DMA
    f32 = jnp.float32
    wide = pltpu.CompilerParams(vmem_limit_bytes=32 * 1024 * 1024)
    on_chip = pl.BlockSpec(memory_space=pltpu.VMEM)
    in_hbm = pl.BlockSpec(memory_space=pltpu.HBM)
    anywhere = pl.BlockSpec(memory_space=pl.ANY)
    advanced, inflow = pl.pallas_call(
        functools.partial(kernel, n),
        name="lattice",
        out_shape=(
            pltpu.VMEM(populations.shape, f32),
            pltpu.VMEM((3, STEPS, local), f32),
        ),
        in_specs=[pl.BlockSpec(memory_space=pltpu.SMEM)] + [in_hbm] * 6,
        out_specs=(on_chip, on_chip),
        scratch_shapes=[
            pltpu.VMEM((1, inlet_cells.shape[0]), jnp.int32),
            pltpu.VMEM((3, local, modes), f32),
            pltpu.VMEM((3, mri_frames.shape[0], local), f32),
            pltpu.VMEM((height, inlet_cells.shape[0]), jnp.bfloat16),
            pltpu.VMEM((width, inlet_cells.shape[0]), jnp.bfloat16),
            pltpu.VMEM((planes, height, width), jnp.int32),
            pltpu.VMEM((2, planes, height, width), jnp.int32),
            pltpu.VMEM((STEPS, 19, planes, height + 2 * PAD, width), f32),
            pltpu.VMEM((STEPS, CROSS, height + 2 * PAD, width), f32),
            pltpu.VMEM((STEPS, CROSS, height + 2 * PAD, width), f32),
            pltpu.VMEM((STEPS, modes), f32),
            pltpu.VMEM((n - 1, STEPS, modes), f32),
            pltpu.VMEM((3, STEPS, LANES), f32),
            pltpu.VMEM((n - 1, 3, STEPS, LANES), f32),
            dma((planes,)),
            dma((5,)),
            dma((1,)),
            dma((1,)),
            dma((1,)),
            dma((1,)),
            dma((STEPS,)),
            dma((STEPS,)),
            dma((STEPS,)),
            dma((STEPS,)),
        ],
        compiler_params=pltpu.CompilerParams(
            collective_id=0, has_side_effects=True, vmem_limit_bytes=32 * 1024 * 1024
        ),
    )(
        frame_index,
        *(
            pltpu.with_memory_space_constraint(operand, pltpu.HBM)
            for operand in (
                populations,
                solid_mask,
                link_flags,
                inlet_cells.reshape(1, -1),
                jnp.transpose(pod_basis, (1, 2, 0)),
                jnp.transpose(mri_frames, (1, 0, 2)),
            )
        )
    )
    advanced, inflow = pl.pallas_call(
        finish,
        name="finish",
        out_shape=(
            jax.ShapeDtypeStruct(populations.shape, f32),
            jax.ShapeDtypeStruct((3, STEPS, local), f32),
        ),
        in_specs=[on_chip, on_chip],
        out_specs=(anywhere, anywhere),
        scratch_shapes=[dma((2,))],
        compiler_params=wide,
    )(advanced, inflow)
    return advanced, jnp.transpose(inflow, (1, 0, 2))


def solution(mesh):
    in_specs = (
        P(None, "ax", "case", None),
        P("ax", "case", None),
        P(None, "ax", "case", None),
        P("case"),
        P(None, None, "ax"),
        P(None, "case", "ax"),
        P(),
    )
    out_specs = (P(None, "ax", "case", None), P(None, "case", "ax"))
    return jax.shard_map(
        functools.partial(body, mesh.shape["ax"]),
        mesh=mesh,
        in_specs=in_specs,
        out_specs=out_specs,
        check_vma=False,
    )
```
